1024 devices in a mesh: lat: 32 (over x, y), lev: 32 (over z, core).
Axes of the slice: x: 4, y: 8, z: 16, core: 2. Of those that a mesh axis runs over, the one named last changes fastest.
Arguments:
- grid_gradient: float32 [64, 640, 1280], P('lev', 'lat'), may hold values from -0.4375 to 0.4375
- legendre: bfloat16 [640, 640, 320], P('lat', 'lev'), may hold values from -0.15625 to 0.15625
- assign: int32 [640], replicated, may hold values from 0 to 639, as said below
Outputs:
- coeff_gradient: bfloat16 [640, 640, 128], P('lat', 'lev')
The draws below stay inside these ranges and needn't reach their ends.
Inputs may be any that keep to these rules, and one draw needn't show every extreme that they name: `assign`: each wavenumber appears once; slots 2q and 2q + 1 hold two wavenumbers that sum to 639.
All inputs are finite; a program needn't handle non-finite values.
Results may differ from the reference program's by a relative error of at most 0.0059.
Values may be sent and summed in bfloat16 or wider, within the bound.
A program may use at most 32 MiB of HBM per device.

```python
import jax
import jax.numpy as jnp
from jax import lax

M = 640
NLAT = 640
NLON = 1280
NH = 320
FL = 64


def draw_assign(key, part):
    pairs = jax.random.permutation(jax.random.fold_in(key, 11), M // 2).astype(jnp.int32)
    flips = jax.random.randint(jax.random.fold_in(key, 12), (M // 2,), 0, 2).astype(jnp.int32)
    upper = (M - 1 - pairs).astype(jnp.int32)
    first = jnp.where(flips == 1, upper, pairs)
    second = jnp.where(flips == 1, pairs, upper)
    return jnp.stack([first, second], axis=1).reshape(M).astype(jnp.int32)


def levels(key, extent, shards, low, high):
    gain, own = 1.0, jax.random.fold_in(key, 6)
    for position, parts in shards:
        draws = jnp.exp(jax.random.uniform(jax.random.fold_in(own, position), (parts,), jnp.float32, low / len(shards), high / len(shards)))
        gain = gain * jnp.repeat(draws, extent[position] // parts).reshape([-1 if axis == position else 1 for axis in range(len(extent))])
    return gain


def normal_values(own_key, extent, width, limit, cuts=(), held_as=jnp.bfloat16):
    factor_of = levels(own_key, extent, cuts, -0.22, 0.18) if cuts else 1.0
    values = jax.random.normal(own_key, extent, jnp.float32) * width * factor_of
    return jnp.minimum(jnp.maximum(values, -limit), limit).astype(held_as)


def setup_inputs(seed: int = 0) -> dict:
    keys = jax.random.split(jax.random.key(seed), 4)
    grid_gradient = normal_values(keys[0], (FL, NLAT, NLON), 0.03, 0.4375, ((0, 32), (1, 32)), jnp.float32)
    legendre = normal_values(keys[1], (M, M, NH), (2 * M) ** -0.5, 0.15625, ((0, 32), (1, 32)))
    assign = draw_assign(jax.random.fold_in(keys[3], 71), 0)
    return dict(grid_gradient=grid_gradient, legendre=legendre, assign=assign)


def reference(grid_gradient, legendre, assign):
    transform = jnp.fft.rfft(grid_gradient, axis=-1)[..., :M]
    modes = jnp.arange(M)
    weight = jnp.where(modes == 0, 1.0, 2.0).astype(jnp.float32)
    real_part = jnp.real(transform).astype(jnp.float32) * weight
    imag_part = jnp.imag(transform).astype(jnp.float32) * weight
    spec = jnp.stack([real_part, imag_part], axis=1).astype(jnp.bfloat16)
    north = spec[:, :, :NH, :].astype(jnp.float32)
    south = spec[:, :, ::-1, :][:, :, :NH, :].astype(jnp.float32)
    even = (north + south).astype(jnp.bfloat16)
    odd = (north - south).astype(jnp.bfloat16)
    degrees = jnp.arange(M)

    def one_slot(index):
        wave = assign[index]
        even_col = jnp.take(even, wave, axis=3)
        odd_col = jnp.take(odd, wave, axis=3)
        even_mat = jnp.transpose(even_col, (1, 0, 2)).reshape(2 * FL, NH)
        odd_mat = jnp.transpose(odd_col, (1, 0, 2)).reshape(2 * FL, NH)
        table = legendre[index]
        from_even = jnp.dot(table, even_mat.T, preferred_element_type=jnp.float32)
        from_odd = jnp.dot(table, odd_mat.T, preferred_element_type=jnp.float32)
        chosen = jnp.where((degrees % 2 == 0)[:, None], from_even, from_odd)
        valid = degrees < (M - wave)
        return jnp.where(valid[:, None], chosen, 0.0).astype(jnp.bfloat16)

    return lax.map(one_slot, jnp.arange(M).astype(jnp.int32))
```

```python
import functools

import jax
import jax.numpy as jnp
import numpy as np
from jax import lax
from jax.experimental import pallas as pl
from jax.experimental.pallas import tpu as pltpu
from jax.sharding import PartitionSpec as P

MESH = pl.DeviceIdType.MESH
LANES = 128
ROWS = 20
HALF = 10
KAPPA = 5
PAIRS = HALF // 2
DEG = 24
NT = (((1,), (1,)), ((), ()))


def dot_nt(a, b):
    return lax.dot_general(a, b, NT, preferred_element_type=jnp.float32)


def dot(a, b):
    return jnp.dot(a, b, preferred_element_type=jnp.float32)


def iota(shape, axis):
    return lax.broadcasted_iota(jnp.int32, shape, axis)


def kernel(
    n_lat, n_z, g_ref, leg_ref, asg_ref, tab_hbm, out_ref,
    tab, grid, spec, asg_col, send32, send, recv, mixed, leg32, w_own, w_send, w_part, units, first, p_send, p_recv,
    tab_sem, a_send_sem, a_recv_sem, local_sem, w_sems, p_sems, u_send_sem, u_recv_sem,
):
    modes = n_lat * ROWS
    wide = modes
    half = wide // 2
    dests = 2 * n_lat
    lat = lax.axis_index("lat")
    lev = lax.axis_index("lev")
    z, core = lev // 2, lev % 2
    other = 1 - core
    right = ((z + 1) % n_z) * 2 + core
    left = ((z + n_z - 1) % n_z) * 2 + core
    partner = z * 2 + other
    me = lat * 2 + core

    barrier = pltpu.get_barrier_semaphore()

    def greet(target_lat, target_lev):
        pl.semaphore_signal(barrier, inc=1, device_id={"lat": target_lat, "lev": target_lev}, device_id_type=MESH)

    greet(lat, right)
    greet(lat, left)
    greet(lat, partner)

    def greet_all(step, carry):
        target = (lat + step) % n_lat
        greet(target, z * 2)
        greet(target, z * 2 + 1)
        return carry

    lax.fori_loop(1, n_lat, greet_all, 0)

    quarter = modes // 2
    tab_copies = []
    for i in range(4):
        rows = pl.ds(i * quarter, quarter)
        copy = pltpu.make_async_copy(tab_hbm.at[rows], tab.at[rows], tab_sem.at[i])
        copy.start()
        tab_copies.append(copy)

    for f in range(2):
        value = g_ref[f]
        high = value.astype(jnp.bfloat16).astype(jnp.float32)
        grid[f * DEG : f * DEG + ROWS, :] = high
        grid[64 + f * DEG : 64 + f * DEG + ROWS, :] = value - high
    both = grid[...].astype(jnp.bfloat16)

    for t in range(asg_ref.shape[0]):
        row = jnp.broadcast_to(asg_ref[t : t + 1, :].astype(jnp.float32), (LANES, LANES))
        asg_col[t * LANES : (t + 1) * LANES, :] = jnp.transpose(row)

    for i in range(4):
        tab_copies[i].wait()
        part = dot_nt(tab[i * quarter : (i + 1) * quarter, :], both)
        total = part + pltpu.roll(part, 64, 1)
        c, r = i // 2, (i % 2) * quarter
        spec[r : r + quarter, c * LANES : (c + 1) * LANES] = total.astype(jnp.bfloat16)

    picked = 2 * dests
    lane = iota((picked, LANES), 1)
    tiles = -(-modes // LANES)
    mode_of = iota((picked, modes), 1).astype(jnp.float32)
    packed = [[jnp.zeros((picked, LANES), jnp.float32) for _ in range(2)] for _ in range(2)]
    for kappa in range(KAPPA):
        wave = asg_col[pl.ds(kappa, picked, stride=KAPPA), :]
        wave = jnp.concatenate([wave] * tiles, axis=1)[:, :modes]
        choice = jnp.where(wave == mode_of, 1.0, 0.0).astype(jnp.bfloat16)
        chosen = dot(choice, spec[...])
        here = (lane >= kappa * ROWS) & (lane < (kappa + 1) * ROWS)
        for f in range(2):
            for c in range(2):
                moved = chosen[:, c * LANES : (c + 1) * LANES]
                shift = (kappa * ROWS - f * DEG) % LANES
                if shift:
                    moved = pltpu.roll(moved, shift, 1)
                packed[f][c] = jnp.where(here, moved, packed[f][c])
    for f in range(2):
        for c in range(2):
            send32[pl.ds(f * 2 + c, picked, stride=4), :] = packed[f][c]
    send[...] = send32[...].reshape(dests, 8, LANES).astype(jnp.bfloat16)

    pl.semaphore_wait(barrier, 2 * n_lat - 1 + 2)

    def block_to(target_lat, h):
        pltpu.make_async_remote_copy(
            src_ref=send.at[target_lat * 2 + h],
            dst_ref=recv.at[me],
            send_sem=a_send_sem,
            recv_sem=a_recv_sem,
            device_id={"lat": target_lat, "lev": z * 2 + h},
            device_id_type=MESH,
        ).start()

    def blocks_to(step, carry):
        target = (lat + step) % n_lat
        block_to(target, 0)
        block_to(target, 1)
        return carry

    lax.fori_loop(1, n_lat, blocks_to, 0)
    block_to(lat, other)
    own_block = pltpu.make_async_copy(send.at[me], recv.at[me], local_sem)
    own_block.start()

    for s in range(ROWS):
        leg32[s * DEG : s * DEG + ROWS, :] = leg_ref[s].astype(jnp.float32)
    row_of = iota((half, wide), 0)
    col_of = iota((half, wide), 1)
    mirror = jnp.where((row_of == col_of) | (row_of + col_of == wide - 1), 1.0, 0.0).astype(jnp.bfloat16)
    degree = iota((DEG, wide), 0)
    sign = jnp.where((degree % 2 == 1) & (iota((DEG, wide), 1) >= half), -1.0, 1.0)
    degree = degree.astype(jnp.float32)

    def factors(h, p, ref):
        pair = []
        first_slot = h * HALF + 2 * p
        source = leg32[pl.ds(pl.multiple_of(first_slot * DEG, 8), 2 * DEG), :].astype(jnp.bfloat16)
        spread = dot(source, mirror)
        for s in range(2):
            wave = asg_col[pl.ds(lat * ROWS + first_slot + s, 1), :]
            wave = jnp.concatenate([wave] * tiles, axis=1)[:, :modes]
            limit = jnp.minimum(modes - wave - (lev * ROWS).astype(jnp.float32), float(ROWS))
            keep = degree < jnp.broadcast_to(limit, (DEG, wide))
            pair.append(jnp.where(keep, spread[s * DEG : (s + 1) * DEG] * sign, 0.0))
        ref[p] = jnp.concatenate(pair, axis=0).astype(jnp.bfloat16)

    for p in range(PAIRS):
        factors(other, p, w_send)
    w_copy = pltpu.make_async_remote_copy(
        src_ref=w_send, dst_ref=w_part, send_sem=w_sems.at[0], recv_sem=w_sems.at[1],
        device_id={"lat": lat, "lev": partner}, device_id_type=MESH,
    )
    w_copy.start()
    for p in range(PAIRS):
        factors(core, p, w_own)

    src = iota((n_z * 16, 2 * n_z * 8), 0)
    dst = iota((n_z * 16, 2 * n_z * 8), 1)
    position, inner = src // 16, src % 16
    away = (position + 1) // 2
    from_z = jnp.where(position % 2 == 1, z - away + n_z, z + away) % n_z
    field = from_z * 4 + (inner % 8) // 2
    column = (inner // 8) * (n_z * 8) + (inner % 2) * (n_z * 4) + field
    place = jnp.where(column == dst, 1.0, 0.0).astype(jnp.bfloat16)

    pltpu.make_async_copy(recv.at[pl.ds(0, dests - 1)], recv.at[pl.ds(0, dests - 1)], a_recv_sem).wait()
    own_block.wait()
    low = iota((8, LANES), 0) < 4
    for i in range(n_lat):
        a = recv[2 * i].astype(jnp.float32)
        b = recv[2 * i + 1].astype(jnp.float32)
        mixed[0, i] = jnp.where(low, a, pltpu.roll(b, 4, 0))
        mixed[1, i] = jnp.where(low, pltpu.roll(a, 4, 0), b)

    lane = iota((8, LANES), 1)

    def side_by_side(slot):
        u, kappa = slot // KAPPA, slot % KAPPA
        parts = [jnp.zeros((8, LANES), jnp.float32) for _ in range(tiles)]
        for i in range(n_lat):
            start = i * ROWS
            t, offset = start // LANES, start % LANES
            value = mixed[u, i]
            shift = (offset - kappa * ROWS) % LANES
            if shift:
                value = pltpu.roll(value, shift, 1)
            parts[t] = jnp.where((lane >= offset) & (lane < offset + ROWS), value, parts[t])
            if offset + ROWS > LANES:
                parts[t + 1] = jnp.where(lane < offset + ROWS - LANES, value, parts[t + 1])
        return jnp.concatenate(parts, axis=1)[:, :wide]

    def unit_copy(source, target, p, device):
        rows = pl.ds(p * 16, 16)
        return pltpu.make_async_remote_copy(
            src_ref=units.at[source, rows],
            dst_ref=units.at[target, rows],
            send_sem=u_send_sem,
            recv_sem=u_recv_sem.at[target, p],
            device_id={"lat": lat, "lev": device},
            device_id_type=MESH,
        )

    last = n_z - 1

    def pass_right(step, p):
        source = 0 if step == 0 else 2 * step - 1
        if step + 1 < n_z // 2:
            unit_copy(source, 2 * step + 1, p, right).start()
        elif step + 1 == n_z // 2 and p < 3:
            unit_copy(source, last, p, right).start()

    def pass_left(step, p):
        source = 2 * step
        if step + 1 < n_z // 2:
            unit_copy(source, 2 * step + 2, p, left).start()
        elif step + 1 == n_z // 2 and p >= 3:
            unit_copy(source, last, p, left).start()

    for p in range(PAIRS):
        rows = jnp.concatenate([side_by_side(2 * p), side_by_side(2 * p + 1)], axis=0)
        units[0, p * 16 : (p + 1) * 16, :] = rows.astype(jnp.bfloat16)
        pass_right(0, p)
        pass_left(0, p)

    w_copy.wait()

    def contract(p, begin, end):
        arrived = units[begin:end, p * 16 : (p + 1) * 16, :].reshape((end - begin) * 16, wide)
        factor = jnp.concatenate([w_own[p], w_part[p]], axis=0)
        return dot_nt(factor, arrived).astype(jnp.bfloat16)

    middle = n_z // 2
    for step in range(1, n_z // 2):
        for p in range(PAIRS):
            unit_copy(0, 2 * step - 1, p, right).wait_recv()
            pass_right(step, p)
            unit_copy(0, 2 * step, p, left).wait_recv()
            pass_left(step, p)
            if step == n_z // 4:
                first[p] = contract(p, 0, middle)
    for p in range(PAIRS):
        unit_copy(0, last, p, right).wait_recv()
        second = contract(p, middle, n_z)
        product = dot(jnp.concatenate([first[p], second], axis=1), place)
        width = n_z * 8
        for s in range(2):
            lanes = slice(s * width, (s + 1) * width)
            mine = product[s * DEG : s * DEG + ROWS, lanes].astype(jnp.bfloat16)
            out_ref[core * HALF + 2 * p + s] = mine
            theirs = product[(2 + s) * DEG : (3 + s) * DEG, lanes].astype(jnp.bfloat16)
            p_send[2 * p + s] = theirs

    p_copy = pltpu.make_async_remote_copy(
        src_ref=p_send, dst_ref=p_recv, send_sem=p_sems.at[0], recv_sem=p_sems.at[1],
        device_id={"lat": lat, "lev": partner}, device_id_type=MESH,
    )
    p_copy.start()
    pltpu.make_async_copy(send.at[pl.ds(0, dests - 1)], send.at[pl.ds(0, dests - 1)], a_send_sem).wait()
    pltpu.make_async_copy(units.at[pl.ds(0, last)], units.at[pl.ds(0, last)], u_send_sem).wait()
    p_copy.wait()
    for s in range(HALF):
        out_ref[other * HALF + s] = p_recv[s][:ROWS, :]


def table_of(modes, nlon):
    phase = np.arange(modes, dtype=np.int64)[:, None] * np.arange(nlon, dtype=np.int64)[None, :] % nlon
    angle = phase * (2.0 * np.pi / nlon)
    weight = np.where(np.arange(modes) == 0, 1.0, 2.0)[:, None]
    return np.concatenate([np.cos(angle) * weight, -np.sin(angle) * weight], axis=0)


def per_device(n_lat, n_z, grid_gradient, legendre, assign):
    modes = n_lat * ROWS
    nlon = grid_gradient.shape[2]
    wide, half, dests = modes, modes // 2, 2 * n_lat
    tiles = -(-modes // LANES)
    table = jnp.asarray(table_of(modes, nlon).astype(jnp.bfloat16))
    rows = jnp.pad(assign, (0, tiles * LANES - modes)).reshape(tiles, LANES)
    vmem = pl.BlockSpec(memory_space=pltpu.VMEM)
    bf16, f32 = jnp.bfloat16, jnp.float32
    dma = pltpu.SemaphoreType.DMA
    return pl.pallas_call(
        functools.partial(kernel, n_lat, n_z),
        out_shape=jax.ShapeDtypeStruct((ROWS, ROWS, n_z * 8), bf16),
        in_specs=[vmem, vmem, vmem, pl.BlockSpec(memory_space=pltpu.MemorySpace.HBM)],
        out_specs=vmem,
        scratch_shapes=[
            pltpu.VMEM((2 * modes, nlon), bf16),
            pltpu.VMEM((LANES, nlon), f32),
            pltpu.VMEM((modes, 2 * LANES), bf16),
            pltpu.VMEM((tiles * LANES, LANES), f32),
            pltpu.VMEM((dests * 8, LANES), f32),
            pltpu.VMEM((dests, 8, LANES), bf16),
            pltpu.VMEM((dests, 8, LANES), bf16),
            pltpu.VMEM((2, n_lat, 8, LANES), f32),
            pltpu.VMEM((ROWS * DEG, half), f32),
            pltpu.VMEM((PAIRS, 2 * DEG, wide), bf16),
            pltpu.VMEM((PAIRS, 2 * DEG, wide), bf16),
            pltpu.VMEM((PAIRS, 2 * DEG, wide), bf16),
            pltpu.VMEM((n_z, HALF * 8, wide), bf16),
            pltpu.VMEM((PAIRS, 4 * DEG, n_z * 8), bf16),
            pltpu.VMEM((HALF, DEG, n_z * 8), bf16),
            pltpu.VMEM((HALF, DEG, n_z * 8), bf16),
            dma((4,)),
            dma,
            dma,
            dma,
            dma((2,)),
            dma((2,)),
            dma,
            dma((n_z, PAIRS)),
        ],
        compiler_params=pltpu.CompilerParams(collective_id=0, has_side_effects=True),
        name="spectral_adjoint",
    )(grid_gradient, legendre, rows, table)


def solution(mesh):
    in_specs = (P("lev", "lat", None), P("lat", "lev", None), P())
    out_specs = P("lat", "lev", None)
    body = functools.partial(per_device, mesh.shape["lat"], mesh.shape["lev"] // 2)
    return jax.shard_map(body, mesh=mesh, in_specs=in_specs, out_specs=out_specs, check_vma=False)
```

```python
import functools

import jax
import jax.numpy as jnp
import numpy as np
from jax import lax
from jax.experimental import pallas as pl
from jax.experimental.pallas import tpu as pltpu
from jax.sharding import PartitionSpec as P

MESH = pl.DeviceIdType.MESH
LANES = 128
ROWS = 20
HALF = 10
KAPPA = 5
PAIRS = HALF // 2
DEG = 24
NT = (((1,), (1,)), ((), ()))


def dot_nt(a, b):
    return lax.dot_general(a, b, NT, preferred_element_type=jnp.float32)


def dot(a, b):
    return jnp.dot(a, b, preferred_element_type=jnp.float32)


def iota(shape, axis):
    return lax.broadcasted_iota(jnp.int32, shape, axis)


def kernel(
    n_lat, n_z, g_ref, leg_ref, asg_ref, tab_hbm, out_ref,
    tab, grid, both, spec, asg_col, send32, send, recv, mixed, leg32, w_own, w_send, w_part, units, first, p_send, p_recv,
    tab_sem, a_send_sem, a_recv_sem, local_sem, w_sems, p_sems, u_send_sem, u_recv_sem,
):
    modes = n_lat * ROWS
    wide = modes
    half = wide // 2
    nlon = tab.shape[1]
    dests = 2 * n_lat
    lat = lax.axis_index("lat")
    lev = lax.axis_index("lev")
    z, core = lev // 2, lev % 2
    other = 1 - core
    right = ((z + 1) % n_z) * 2 + core
    left = ((z + n_z - 1) % n_z) * 2 + core
    partner = z * 2 + other
    me = lat * 2 + core

    barrier = pltpu.get_barrier_semaphore()

    def greet(target_lat, target_lev):
        pl.semaphore_signal(barrier, inc=1, device_id={"lat": target_lat, "lev": target_lev}, device_id_type=MESH)

    greet(lat, right)
    greet(lat, left)
    greet(lat, partner)

    def greet_all(step, carry):
        target = (lat + step) % n_lat
        greet(target, z * 2)
        greet(target, z * 2 + 1)
        return carry

    lax.fori_loop(1, n_lat, greet_all, 0)

    kept = tab.shape[0] // 2
    split = kept // 32 * 16
    pieces = [(0, 0, split), (0, split, kept), (1, 0, split), (1, split, kept)]
    tab_copies = []
    for i, (c, begin, end) in enumerate(pieces):
        rows = pl.ds(c * kept + begin, end - begin)
        copy = pltpu.make_async_copy(tab_hbm.at[rows], tab.at[rows], tab_sem.at[i])
        copy.start()
        tab_copies.append(copy)

    for f in range(2):
        value = g_ref[:, f, :]
        high = value.astype(jnp.bfloat16).astype(jnp.float32)
        grid[f * DEG : f * DEG + ROWS, :] = high
        grid[64 + f * DEG : 64 + f * DEG + ROWS, :] = value - high
    down = jnp.transpose(grid[...])
    turn = jnp.where(iota(down.shape, 0) % 2 == 1, -1.0, 1.0)
    both[...] = jnp.concatenate([down, down * turn], axis=1).astype(jnp.bfloat16)

    for t in range(asg_ref.shape[0]):
        row = jnp.broadcast_to(asg_ref[t : t + 1, :].astype(jnp.float32), (LANES, LANES))
        asg_col[t * LANES : (t + 1) * LANES, :] = jnp.transpose(row)

    for i, (c, begin, end) in enumerate(pieces):
        tab_copies[i].wait()
        part = dot(tab[c * kept + begin : c * kept + end, :], both[...])
        for turned in range(2):
            half_part = part[:, turned * LANES : (turned + 1) * LANES]
            total = half_part + pltpu.roll(half_part, 64, 1)
            if turned and c:
                total = -total
            begins = turned * kept + begin
            spec[begins : begins + end - begin, c * LANES : (c + 1) * LANES] = total.astype(jnp.bfloat16)

    picked = 2 * dests
    lane = iota((picked, LANES), 1)
    tiles = -(-modes // LANES)
    entry = iota((picked, 2 * kept), 1)
    mirrored = nlon // 2 - (entry - kept)
    mode_of = jnp.where(entry < kept, entry, jnp.where(mirrored >= kept, mirrored, -1)).astype(jnp.float32)
    entry_tiles = -(-2 * kept // LANES)
    packed = [[jnp.zeros((picked, LANES), jnp.float32) for _ in range(2)] for _ in range(2)]
    for kappa in range(KAPPA):
        wave = asg_col[pl.ds(kappa, picked, stride=KAPPA), :]
        wave = jnp.concatenate([wave] * entry_tiles, axis=1)[:, : 2 * kept]
        choice = jnp.where(wave == mode_of, 1.0, 0.0).astype(jnp.bfloat16)
        chosen = dot(choice, spec[...])
        here = (lane >= kappa * ROWS) & (lane < (kappa + 1) * ROWS)
        for f in range(2):
            for c in range(2):
                moved = chosen[:, c * LANES : (c + 1) * LANES]
                shift = (kappa * ROWS - f * DEG) % LANES
                if shift:
                    moved = pltpu.roll(moved, shift, 1)
                packed[f][c] = jnp.where(here, moved, packed[f][c])
    for f in range(2):
        for c in range(2):
            send32[pl.ds(f * 2 + c, picked, stride=4), :] = packed[f][c]
    send[...] = send32[...].reshape(dests, 8, LANES).astype(jnp.bfloat16)

    pl.semaphore_wait(barrier, 2 * n_lat - 1 + 2)

    def block_to(target_lat, h):
        pltpu.make_async_remote_copy(
            src_ref=send.at[target_lat * 2 + h],
            dst_ref=recv.at[me],
            send_sem=a_send_sem,
            recv_sem=a_recv_sem,
            device_id={"lat": target_lat, "lev": z * 2 + h},
            device_id_type=MESH,
        ).start()

    def blocks_to(step, carry):
        target = (lat + step) % n_lat
        block_to(target, 0)
        block_to(target, 1)
        return carry

    lax.fori_loop(1, n_lat, blocks_to, 0)
    block_to(lat, other)
    own_block = pltpu.make_async_copy(send.at[me], recv.at[me], local_sem)
    own_block.start()

    for s in range(ROWS):
        leg32[s * DEG : s * DEG + ROWS, :] = leg_ref[s].astype(jnp.float32)
    row_of = iota((half, wide), 0)
    col_of = iota((half, wide), 1)
    mirror = jnp.where((row_of == col_of) | (row_of + col_of == wide - 1), 1.0, 0.0).astype(jnp.bfloat16)
    degree = iota((DEG, wide), 0)
    sign = jnp.where((degree % 2 == 1) & (iota((DEG, wide), 1) >= half), -1.0, 1.0)
    degree = degree.astype(jnp.float32)

    def factors(h, p, ref):
        pair = []
        first_slot = h * HALF + 2 * p
        source = leg32[pl.ds(pl.multiple_of(first_slot * DEG, 8), 2 * DEG), :].astype(jnp.bfloat16)
        spread = dot(source, mirror)
        for s in range(2):
            wave = asg_col[pl.ds(lat * ROWS + first_slot + s, 1), :]
            wave = jnp.concatenate([wave] * tiles, axis=1)[:, :modes]
            limit = jnp.minimum(modes - wave - (lev * ROWS).astype(jnp.float32), float(ROWS))
            keep = degree < jnp.broadcast_to(limit, (DEG, wide))
            pair.append(jnp.where(keep, spread[s * DEG : (s + 1) * DEG] * sign, 0.0))
        ref[p] = jnp.concatenate(pair, axis=0).astype(jnp.bfloat16)

    for p in range(PAIRS):
        factors(other, p, w_send)
    w_copy = pltpu.make_async_remote_copy(
        src_ref=w_send, dst_ref=w_part, send_sem=w_sems.at[0], recv_sem=w_sems.at[1],
        device_id={"lat": lat, "lev": partner}, device_id_type=MESH,
    )
    w_copy.start()
    for p in range(PAIRS):
        factors(core, p, w_own)

    src = iota((n_z * 16, 2 * n_z * 8), 0)
    dst = iota((n_z * 16, 2 * n_z * 8), 1)
    position, inner = src // 16, src % 16
    away = (position + 1) // 2
    from_z = jnp.where(position % 2 == 1, z - away + n_z, z + away) % n_z
    field = from_z * 4 + (inner % 8) // 2
    column = (inner // 8) * (n_z * 8) + (inner % 2) * (n_z * 4) + field
    place = jnp.where(column == dst, 1.0, 0.0).astype(jnp.bfloat16)

    pltpu.make_async_copy(recv.at[pl.ds(0, dests - 1)], recv.at[pl.ds(0, dests - 1)], a_recv_sem).wait()
    own_block.wait()
    low = iota((8, LANES), 0) < 4
    for i in range(n_lat):
        a = recv[2 * i].astype(jnp.float32)
        b = recv[2 * i + 1].astype(jnp.float32)
        mixed[0, i] = jnp.where(low, a, pltpu.roll(b, 4, 0))
        mixed[1, i] = jnp.where(low, pltpu.roll(a, 4, 0), b)

    lane = iota((8, LANES), 1)

    def side_by_side(slot):
        u, kappa = slot // KAPPA, slot % KAPPA
        parts = [jnp.zeros((8, LANES), jnp.float32) for _ in range(tiles)]
        for i in range(n_lat):
            start = i * ROWS
            t, offset = start // LANES, start % LANES
            value = mixed[u, i]
            shift = (offset - kappa * ROWS) % LANES
            if shift:
                value = pltpu.roll(value, shift, 1)
            parts[t] = jnp.where((lane >= offset) & (lane < offset + ROWS), value, parts[t])
            if offset + ROWS > LANES:
                parts[t + 1] = jnp.where(lane < offset + ROWS - LANES, value, parts[t + 1])
        return jnp.concatenate(parts, axis=1)[:, :wide]

    def unit_copy(source, target, p, device):
        rows = pl.ds(p * 16, 16)
        return pltpu.make_async_remote_copy(
            src_ref=units.at[source, rows],
            dst_ref=units.at[target, rows],
            send_sem=u_send_sem,
            recv_sem=u_recv_sem.at[target, p],
            device_id={"lat": lat, "lev": device},
            device_id_type=MESH,
        )

    last = n_z - 1

    def pass_right(step, p):
        source = 0 if step == 0 else 2 * step - 1
        if step + 1 < n_z // 2:
            unit_copy(source, 2 * step + 1, p, right).start()
        elif step + 1 == n_z // 2 and p < 3:
            unit_copy(source, last, p, right).start()

    def pass_left(step, p):
        source = 2 * step
        if step + 1 < n_z // 2:
            unit_copy(source, 2 * step + 2, p, left).start()
        elif step + 1 == n_z // 2 and p >= 3:
            unit_copy(source, last, p, left).start()

    for p in range(PAIRS):
        rows = jnp.concatenate([side_by_side(2 * p), side_by_side(2 * p + 1)], axis=0)
        units[0, p * 16 : (p + 1) * 16, :] = rows.astype(jnp.bfloat16)
        pass_right(0, p)
        pass_left(0, p)

    w_copy.wait()

    def contract(p, begin, end):
        arrived = units[begin:end, p * 16 : (p + 1) * 16, :].reshape((end - begin) * 16, wide)
        factor = jnp.concatenate([w_own[p], w_part[p]], axis=0)
        columns = dot_nt(factor, arrived).astype(jnp.bfloat16)
        return dot(columns, place[begin * 16 : end * 16])

    ends = {n_z // 4: n_z // 2, n_z * 3 // 8: n_z * 3 // 4 + 1, n_z // 2 - 1: last}
    done = 0
    for step in range(1, n_z // 2):
        for p in range(PAIRS):
            unit_copy(0, 2 * step - 1, p, right).wait_recv()
            pass_right(step, p)
            unit_copy(0, 2 * step, p, left).wait_recv()
            pass_left(step, p)
        if step in ends:
            for p in range(PAIRS):
                value = contract(p, done, ends[step])
                first[p] = value if done == 0 else first[p] + value
            done = ends[step]
    for p in range(PAIRS):
        unit_copy(0, last, p, right).wait_recv()
        product = first[p] + contract(p, done, n_z)
        width = n_z * 8
        for s in range(2):
            lanes = slice(s * width, (s + 1) * width)
            mine = product[s * DEG : s * DEG + ROWS, lanes].astype(jnp.bfloat16)
            out_ref[core * HALF + 2 * p + s] = mine
            theirs = product[(2 + s) * DEG : (3 + s) * DEG, lanes].astype(jnp.bfloat16)
            p_send[2 * p + s] = theirs

    p_copy = pltpu.make_async_remote_copy(
        src_ref=p_send, dst_ref=p_recv, send_sem=p_sems.at[0], recv_sem=p_sems.at[1],
        device_id={"lat": lat, "lev": partner}, device_id_type=MESH,
    )
    p_copy.start()
    pltpu.make_async_copy(send.at[pl.ds(0, dests - 1)], send.at[pl.ds(0, dests - 1)], a_send_sem).wait()
    pltpu.make_async_copy(units.at[pl.ds(0, last)], units.at[pl.ds(0, last)], u_send_sem).wait()
    p_copy.wait()
    for s in range(HALF):
        out_ref[other * HALF + s] = p_recv[s][:ROWS, :]


def table_of(kept, nlon):
    phase = np.arange(kept, dtype=np.int64)[:, None] * np.arange(nlon, dtype=np.int64)[None, :] % nlon
    angle = phase * (2.0 * np.pi / nlon)
    weight = np.where(np.arange(kept) == 0, 1.0, 2.0)[:, None]
    return np.concatenate([np.cos(angle) * weight, -np.sin(angle) * weight], axis=0)


def per_device(n_lat, n_z, grid_gradient, legendre, assign):
    modes = n_lat * ROWS
    nlon = grid_gradient.shape[2]
    wide, half, dests = modes, modes // 2, 2 * n_lat
    tiles = -(-modes // LANES)
    kept = (nlon // 4 + 16) // 16 * 16
    table = jnp.asarray(table_of(kept, nlon).astype(jnp.bfloat16))
    rows = jnp.pad(assign, (0, tiles * LANES - modes)).reshape(tiles, LANES)
    vmem = pl.BlockSpec(memory_space=pltpu.VMEM)
    bf16, f32 = jnp.bfloat16, jnp.float32
    dma = pltpu.SemaphoreType.DMA
    result = pl.pallas_call(
        functools.partial(kernel, n_lat, n_z),
        out_shape=pltpu.VMEM((ROWS, ROWS, n_z * 8), bf16),
        in_specs=[vmem, vmem, vmem, pl.BlockSpec(memory_space=pltpu.MemorySpace.HBM)],
        out_specs=vmem,
        scratch_shapes=[
            pltpu.VMEM((2 * kept, nlon), bf16),
            pltpu.VMEM((LANES, nlon), f32),
            pltpu.VMEM((nlon, 2 * LANES), bf16),
            pltpu.VMEM((2 * kept, 2 * LANES), bf16),
            pltpu.VMEM((tiles * LANES, LANES), f32),
            pltpu.VMEM((dests * 8, LANES), f32),
            pltpu.VMEM((dests, 8, LANES), bf16),
            pltpu.VMEM((dests, 8, LANES), bf16),
            pltpu.VMEM((2, n_lat, 8, LANES), f32),
            pltpu.VMEM((ROWS * DEG, half), f32),
            pltpu.VMEM((PAIRS, 2 * DEG, wide), bf16),
            pltpu.VMEM((PAIRS, 2 * DEG, wide), bf16),
            pltpu.VMEM((PAIRS, 2 * DEG, wide), bf16),
            pltpu.VMEM((n_z, HALF * 8, wide), bf16),
            pltpu.VMEM((PAIRS, 4 * DEG, 2 * n_z * 8), f32),
            pltpu.VMEM((HALF, DEG, n_z * 8), bf16),
            pltpu.VMEM((HALF, DEG, n_z * 8), bf16),
            dma((4,)),
            dma,
            dma,
            dma,
            dma((2,)),
            dma((2,)),
            dma,
            dma((n_z, PAIRS)),
        ],
        compiler_params=pltpu.CompilerParams(collective_id=0, has_side_effects=True),
        name="spectral_adjoint",
    )(jnp.transpose(grid_gradient, (1, 0, 2)), legendre, rows, table)

    def hand_on(result_ref, out_ref):
        out_ref[...] = result_ref[...]

    return pl.pallas_call(
        hand_on,
        out_shape=jax.ShapeDtypeStruct(result.shape, result.dtype),
        in_specs=[vmem],
        out_specs=vmem,
        name="hand_on",
    )(pltpu.with_memory_space_constraint(result, pltpu.VMEM))


def solution(mesh):
    in_specs = (P("lev", "lat", None), P("lat", "lev", None), P())
    out_specs = P("lat", "lev", None)
    body = functools.partial(per_device, mesh.shape["lat"], mesh.shape["lev"] // 2)
    return jax.shard_map(body, mesh=mesh, in_specs=in_specs, out_specs=out_specs, check_vma=False)
```

```python
import functools

import jax
import jax.numpy as jnp
import numpy as np
from jax import lax
from jax.experimental import pallas as pl
from jax.experimental.pallas import tpu as pltpu
from jax.sharding import PartitionSpec as P

MESH = pl.DeviceIdType.MESH
LANES = 128
ROWS = 20
KAPPA = 5
OWN = 5
CHUNKS = (pl.ds(0, 3), pl.ds(3, 2))
DEG = 24
NT = (((1,), (1,)), ((), ()))


def dot_nt(a, b):
    return lax.dot_general(a, b, NT, preferred_element_type=jnp.float32)


def dot(a, b):
    return jnp.dot(a, b, preferred_element_type=jnp.float32)


def iota(shape, axis):
    return lax.broadcasted_iota(jnp.int32, shape, axis)


def kernel(
    n_lat, n_z, g_ref, leg_ref, asg_ref, tab_hbm, out_ref,
    tab, grid, both, spec, asg_col, send32, send, recv, mixed, leg32, l_send, l_recv, spread, factor, units, away, first,
    p_send, p_recv, tab_sem, a_send_sem, a_recv_sem, local_sem, l_sems, p_sems, u_send_sem, u_recv_sem,
):
    modes = n_lat * ROWS
    wide = modes
    half = wide // 2
    nlon = tab.shape[1]
    dests = 2 * n_lat
    lat = lax.axis_index("lat")
    lev = lax.axis_index("lev")
    z, core = lev // 2, lev % 2
    other = 1 - core
    odd = z % 2

    def along(distance):
        return ((z + distance + n_z) % n_z) * 2 + core

    twin = z + 1 - 2 * odd
    partner = z * 2 + other
    team = [(partner, other * 2 + odd), (twin * 2 + core, core * 2 + 1 - odd), (twin * 2 + other, other * 2 + 1 - odd)]
    home = core * 2 + odd
    me = lat * 2 + core

    barrier = pltpu.get_barrier_semaphore()

    def greet(target_lat, target_lev):
        pl.semaphore_signal(barrier, inc=1, device_id={"lat": target_lat, "lev": target_lev}, device_id_type=MESH)

    for distance in (1, -1, 2, -2):
        greet(lat, along(distance))
    greet(lat, partner)
    greet(lat, team[2][0])

    def greet_all(step, carry):
        target = (lat + step) % n_lat
        greet(target, z * 2)
        greet(target, z * 2 + 1)
        return carry

    lax.fori_loop(1, n_lat, greet_all, 0)

    kept = tab.shape[0] // 2
    split = kept // 32 * 16
    pieces = [(0, 0, split), (0, split, kept), (1, 0, split), (1, split, kept)]
    tab_copies = []
    for i, (c, begin, end) in enumerate(pieces):
        rows = pl.ds(c * kept + begin, end - begin)
        copy = pltpu.make_async_copy(tab_hbm.at[rows], tab.at[rows], tab_sem.at[i])
        copy.start()
        tab_copies.append(copy)

    for f in range(2):
        value = g_ref[:, f, :]
        high = value.astype(jnp.bfloat16).astype(jnp.float32)
        grid[f * DEG : f * DEG + ROWS, :] = high
        grid[64 + f * DEG : 64 + f * DEG + ROWS, :] = value - high
    down = jnp.transpose(grid[...])
    turn = jnp.where(iota(down.shape, 0) % 2 == 1, -1.0, 1.0)
    both[...] = jnp.concatenate([down, down * turn], axis=1).astype(jnp.bfloat16)

    for t in range(asg_ref.shape[0]):
        row = jnp.broadcast_to(asg_ref[t : t + 1, :].astype(jnp.float32), (LANES, LANES))
        asg_col[t * LANES : (t + 1) * LANES, :] = jnp.transpose(row)

    for i, (c, begin, end) in enumerate(pieces):
        tab_copies[i].wait()
        part = dot(tab[c * kept + begin : c * kept + end, :], both[...])
        for turned in range(2):
            half_part = part[:, turned * LANES : (turned + 1) * LANES]
            total = half_part + pltpu.roll(half_part, 64, 1)
            if turned and c:
                total = -total
            begins = turned * kept + begin
            spec[begins : begins + end - begin, c * LANES : (c + 1) * LANES] = total.astype(jnp.bfloat16)

    picked = 2 * dests
    lane = iota((picked, LANES), 1)
    tiles = -(-modes // LANES)
    entry = iota((picked, 2 * kept), 1)
    mirrored = nlon // 2 - (entry - kept)
    mode_of = jnp.where(entry < kept, entry, jnp.where(mirrored >= kept, mirrored, -1)).astype(jnp.float32)
    entry_tiles = -(-2 * kept // LANES)
    packed = [[jnp.zeros((picked, LANES), jnp.float32) for _ in range(2)] for _ in range(2)]
    for kappa in range(KAPPA):
        wave = asg_col[pl.ds(kappa, picked, stride=KAPPA), :]
        wave = jnp.concatenate([wave] * entry_tiles, axis=1)[:, : 2 * kept]
        choice = jnp.where(wave == mode_of, 1.0, 0.0).astype(jnp.bfloat16)
        chosen = dot(choice, spec[...])
        here = (lane >= kappa * ROWS) & (lane < (kappa + 1) * ROWS)
        for f in range(2):
            for c in range(2):
                moved = chosen[:, c * LANES : (c + 1) * LANES]
                shift = (kappa * ROWS - f * DEG) % LANES
                if shift:
                    moved = pltpu.roll(moved, shift, 1)
                packed[f][c] = jnp.where(here, moved, packed[f][c])
    for f in range(2):
        for c in range(2):
            send32[pl.ds(f * 2 + c, picked, stride=4), :] = packed[f][c]
    send[...] = send32[...].reshape(dests, 8, LANES).astype(jnp.bfloat16)

    pl.semaphore_wait(barrier, 2 * n_lat - 1 + 5)

    def block_to(target_lat, h):
        pltpu.make_async_remote_copy(
            src_ref=send.at[target_lat * 2 + h],
            dst_ref=recv.at[me],
            send_sem=a_send_sem,
            recv_sem=a_recv_sem,
            device_id={"lat": target_lat, "lev": z * 2 + h},
            device_id_type=MESH,
        ).start()

    def blocks_to(step, carry):
        target = (lat + step) % n_lat
        block_to(target, 0)
        block_to(target, 1)
        return carry

    lax.fori_loop(1, n_lat, blocks_to, 0)
    block_to(lat, other)
    own_block = pltpu.make_async_copy(send.at[me], recv.at[me], local_sem)
    own_block.start()

    for s in range(ROWS):
        leg32[s * DEG : s * DEG + ROWS, :] = leg_ref[s].astype(jnp.float32)
    for group in range(4):
        l_send[group] = leg32[group * OWN * DEG : (group + 1) * OWN * DEG, :].astype(jnp.bfloat16)
    l_copies = []
    for i, (device, group) in enumerate(team):
        copy = pltpu.make_async_remote_copy(
            src_ref=l_send.at[group], dst_ref=l_recv.at[i], send_sem=l_sems.at[i], recv_sem=l_sems.at[3 + i],
            device_id={"lat": lat, "lev": device}, device_id_type=MESH,
        )
        copy.start()
        l_copies.append(copy)

    row_of = iota((half, wide), 0)
    col_of = iota((half, wide), 1)
    mirror = jnp.where((row_of == col_of) | (row_of + col_of == wide - 1), 1.0, 0.0).astype(jnp.bfloat16)

    src = iota((n_z * 8, n_z * 8), 0)
    dst = iota((n_z * 8, n_z * 8), 1)
    position, inner = src // 8, src % 8
    distance = (position + 1) // 2
    from_z = jnp.where(position % 2 == 1, z - distance + n_z, z + distance) % n_z
    column = (inner % 2) * (n_z * 4) + from_z * 4 + inner // 2
    place = jnp.where(column == dst, 1.0, 0.0).astype(jnp.bfloat16)
    spread[0] = dot(l_send[home], mirror)

    pltpu.make_async_copy(recv.at[pl.ds(0, dests - 1)], recv.at[pl.ds(0, dests - 1)], a_recv_sem).wait()
    own_block.wait()
    low = iota((8, LANES), 0) < 4
    for i in range(n_lat):
        a = recv[2 * i].astype(jnp.float32)
        b = recv[2 * i + 1].astype(jnp.float32)
        mixed[0, i] = jnp.where(low, a, pltpu.roll(b, 4, 0))
        mixed[1, i] = jnp.where(low, pltpu.roll(a, 4, 0), b)

    lane = iota((8, LANES), 1)

    def side_by_side(u, kappa):
        parts = [jnp.zeros((8, LANES), jnp.float32) for _ in range(tiles)]
        for i in range(n_lat):
            start = i * ROWS
            t, offset = start // LANES, start % LANES
            value = mixed[u, i]
            shift = (offset - kappa * ROWS) % LANES
            if shift:
                value = pltpu.roll(value, shift, 1)
            parts[t] = jnp.where((lane >= offset) & (lane < offset + ROWS), value, parts[t])
            if offset + ROWS > LANES:
                parts[t + 1] = jnp.where(lane < offset + ROWS - LANES, value, parts[t + 1])
        return jnp.concatenate(parts, axis=1)[:, :wide].astype(jnp.bfloat16)

    def unit_copy(source, target, p, device):
        return pltpu.make_async_remote_copy(
            src_ref=source.at[CHUNKS[p]],
            dst_ref=units.at[target, CHUNKS[p]],
            send_sem=u_send_sem,
            recv_sem=u_recv_sem.at[target, p],
            device_id={"lat": lat, "lev": device},
            device_id_type=MESH,
        )

    last = n_z - 1
    turns = n_z // 2
    right, left = along(2), along(-2)

    def arrive_right(t, p):
        source = 2 * t - 1
        unit_copy(away, source, p, right).wait_recv()
        if t + 2 < turns:
            unit_copy(units.at[source], source + 4, p, right).start()
        elif t + 2 == turns and p == 0:
            unit_copy(units.at[source], last, p, right).start()

    def arrive_left(t, p):
        source = 2 * t
        unit_copy(away, source, p, left).wait_recv()
        if t + 2 < turns:
            unit_copy(units.at[source], source + 4, p, left).start()
        elif t + 2 == turns and p == 1:
            unit_copy(units.at[source], last, p, left).start()

    for p, chunk in enumerate(CHUNKS):
        for kappa in range(chunk.start, chunk.start + chunk.size):
            units[0, kappa] = side_by_side(odd, kappa)
        unit_copy(units.at[0], 3, p, right).start()
        unit_copy(units.at[0], 4, p, left).start()
        for kappa in range(chunk.start, chunk.start + chunk.size):
            away[kappa] = side_by_side(1 - odd, kappa)
        unit_copy(away, 1, p, along(1)).start()
        unit_copy(away, 2, p, along(-1)).start()

    for i in range(3):
        l_copies[i].wait()
        spread[1 + i] = dot(l_recv[i], mirror)
    degree = iota((DEG, wide), 0)
    sign = jnp.where((degree % 2 == 1) & (iota((DEG, wide), 1) >= half), -1.0, 1.0)
    degree = degree.astype(jnp.float32)
    for s in range(OWN):
        wave = asg_col[pl.ds(lat * ROWS + home * OWN + s, 1), :]
        wave = jnp.concatenate([wave] * tiles, axis=1)[:, :modes]
        rows = []
        for i, device in enumerate([lev] + [device for device, _ in team]):
            limit = jnp.minimum(modes - wave - (device * ROWS).astype(jnp.float32), float(ROWS))
            keep = degree < jnp.broadcast_to(limit, (DEG, wide))
            rows.append(jnp.where(keep, spread[i, s * DEG : (s + 1) * DEG, :] * sign, 0.0))
        factor[s] = jnp.concatenate(rows, axis=0).astype(jnp.bfloat16)

    def contract(s, begin, end):
        arrived = units[begin:end, s].astype(jnp.float32).reshape((end - begin) * 8, wide).astype(jnp.bfloat16)
        columns = dot_nt(factor[s], arrived).astype(jnp.bfloat16)
        return dot(columns, place[begin * 8 : end * 8])

    done = 0
    for t in range(1, turns):
        for p in range(2):
            arrive_right(t, p)
            arrive_left(t, p)
        if t in (n_z // 4, n_z * 3 // 8, turns - 1):
            end = (2 * t + 1) // 2 * 2
            for s in range(OWN):
                value = contract(s, done, end)
                first[s] = value if done == 0 else first[s] + value
            done = end
    for p, chunk in enumerate(CHUNKS):
        unit_copy(away, last, p, right).wait_recv()
        for s in range(chunk.start, chunk.start + chunk.size):
            product = first[s] + contract(s, done, n_z)
            out_ref[home * OWN + s] = product[:ROWS].astype(jnp.bfloat16)
            for i in range(3):
                p_send[i, s] = product[(1 + i) * DEG : (2 + i) * DEG].astype(jnp.bfloat16)

    p_copies = []
    for i in (2, 1, 0):
        copy = pltpu.make_async_remote_copy(
            src_ref=p_send.at[i], dst_ref=p_recv.at[i], send_sem=p_sems.at[i], recv_sem=p_sems.at[3 + i],
            device_id={"lat": lat, "lev": team[i][0]}, device_id_type=MESH,
        )
        copy.start()
        p_copies.append((i, copy))
    pltpu.make_async_copy(send.at[pl.ds(0, dests - 1)], send.at[pl.ds(0, dests - 1)], a_send_sem).wait()
    pltpu.make_async_copy(units.at[pl.ds(0, last)], units.at[pl.ds(0, last)], u_send_sem).wait()
    for i, copy in reversed(p_copies):
        copy.wait()
        for s in range(OWN):
            out_ref[team[i][1] * OWN + s] = p_recv[i, s][:ROWS, :]


def table_of(kept, nlon):
    phase = np.arange(kept, dtype=np.int64)[:, None] * np.arange(nlon, dtype=np.int64)[None, :] % nlon
    angle = phase * (2.0 * np.pi / nlon)
    weight = np.where(np.arange(kept) == 0, 1.0, 2.0)[:, None]
    return np.concatenate([np.cos(angle) * weight, -np.sin(angle) * weight], axis=0)


def per_device(n_lat, n_z, grid_gradient, legendre, assign):
    modes = n_lat * ROWS
    nlon = grid_gradient.shape[2]
    wide, half, dests = modes, modes // 2, 2 * n_lat
    tiles = -(-modes // LANES)
    kept = (nlon // 4 + 16) // 16 * 16
    table = jnp.asarray(table_of(kept, nlon).astype(jnp.bfloat16))
    rows = jnp.pad(assign, (0, tiles * LANES - modes)).reshape(tiles, LANES)
    vmem = pl.BlockSpec(memory_space=pltpu.VMEM)
    bf16, f32 = jnp.bfloat16, jnp.float32
    dma = pltpu.SemaphoreType.DMA
    result = pl.pallas_call(
        functools.partial(kernel, n_lat, n_z),
        out_shape=pltpu.VMEM((ROWS, ROWS, n_z * 8), bf16),
        in_specs=[vmem, vmem, vmem, pl.BlockSpec(memory_space=pltpu.MemorySpace.HBM)],
        out_specs=vmem,
        scratch_shapes=[
            pltpu.VMEM((2 * kept, nlon), bf16),
            pltpu.VMEM((LANES, nlon), f32),
            pltpu.VMEM((nlon, 2 * LANES), bf16),
            pltpu.VMEM((2 * kept, 2 * LANES), bf16),
            pltpu.VMEM((tiles * LANES, LANES), f32),
            pltpu.VMEM((dests * 8, LANES), f32),
            pltpu.VMEM((dests, 8, LANES), bf16),
            pltpu.VMEM((dests, 8, LANES), bf16),
            pltpu.VMEM((2, n_lat, 8, LANES), f32),
            pltpu.VMEM((ROWS * DEG, half), f32),
            pltpu.VMEM((4, OWN * DEG, half), bf16),
            pltpu.VMEM((3, OWN * DEG, half), bf16),
            pltpu.VMEM((4, OWN * DEG, wide), f32),
            pltpu.VMEM((OWN, 4 * DEG, wide), bf16),
            pltpu.VMEM((n_z, OWN, 8, wide), bf16),
            pltpu.VMEM((OWN, 8, wide), bf16),
            pltpu.VMEM((OWN, 4 * DEG, n_z * 8), f32),
            pltpu.VMEM((3, OWN, DEG, n_z * 8), bf16),
            pltpu.VMEM((3, OWN, DEG, n_z * 8), bf16),
            dma((4,)),
            dma,
            dma,
            dma,
            dma((6,)),
            dma((6,)),
            dma,
            dma((n_z, 2)),
        ],
        compiler_params=pltpu.CompilerParams(collective_id=0, has_side_effects=True),
        name="spectral_adjoint",
    )(jnp.transpose(grid_gradient, (1, 0, 2)), legendre, rows, table)

    def hand_on(result_ref, out_ref):
        out_ref[...] = result_ref[...]

    return pl.pallas_call(
        hand_on,
        out_shape=jax.ShapeDtypeStruct(result.shape, result.dtype),
        in_specs=[vmem],
        out_specs=vmem,
        name="hand_on",
    )(pltpu.with_memory_space_constraint(result, pltpu.VMEM))


def solution(mesh):
    in_specs = (P("lev", "lat", None), P("lat", "lev", None), P())
    out_specs = P("lat", "lev", None)
    body = functools.partial(per_device, mesh.shape["lat"], mesh.shape["lev"] // 2)
    return jax.shard_map(body, mesh=mesh, in_specs=in_specs, out_specs=out_specs, check_vma=False)
```

```python
import functools

import jax
import jax.numpy as jnp
import numpy as np
from jax import lax
from jax.experimental import pallas as pl
from jax.experimental.pallas import tpu as pltpu
from jax.sharding import PartitionSpec as P

MESH = pl.DeviceIdType.MESH
LANES = 128
ROWS = 20
KAPPA = 5
OWN = 5
CHUNKS = (pl.ds(0, 3), pl.ds(3, 2))
DEG = 24
NT = (((1,), (1,)), ((), ()))


def dot_nt(a, b):
    return lax.dot_general(a, b, NT, preferred_element_type=jnp.float32)


def dot(a, b):
    return jnp.dot(a, b, preferred_element_type=jnp.float32)


def iota(shape, axis):
    return lax.broadcasted_iota(jnp.int32, shape, axis)


def kernel(
    n_lat, n_z, g_ref, leg_ref, asg_ref, tab_hbm, out_ref,
    tab, grid, both, spec, choice, asg_col, send32, send, recv, mixed, leg32, l_send, l_recv, spread, factor, units, away, first,
    p_send, p_recv, tab_sem, a_send_sem, a_recv_sem, local_sem, l_sems, p_sems, u_send_sem, u_recv_sem,
):
    modes = n_lat * ROWS
    wide = modes
    half = wide // 2
    nlon = tab.shape[1]
    dests = 2 * n_lat
    lat = lax.axis_index("lat")
    lev = lax.axis_index("lev")
    z, core = lev // 2, lev % 2
    other = 1 - core
    odd = z % 2

    def along(distance):
        return ((z + distance + n_z) % n_z) * 2 + core

    twin = z + 1 - 2 * odd
    partner = z * 2 + other
    team = [(partner, other * 2 + odd), (twin * 2 + core, core * 2 + 1 - odd), (twin * 2 + other, other * 2 + 1 - odd)]
    home = core * 2 + odd
    me = lat * 2 + core

    kept = tab.shape[0] // 2
    split = kept // 32 * 16
    pieces = [(0, 0, split), (0, split, kept), (1, 0, split), (1, split, kept)]
    tab_copies = []
    for i, (c, begin, end) in enumerate(pieces):
        rows = pl.ds(c * kept + begin, end - begin)
        copy = pltpu.make_async_copy(tab_hbm.at[rows], tab.at[rows], tab_sem.at[i])
        copy.start()
        tab_copies.append(copy)

    barrier = pltpu.get_barrier_semaphore()

    def greet(target_lat, target_lev):
        pl.semaphore_signal(barrier, inc=1, device_id={"lat": target_lat, "lev": target_lev}, device_id_type=MESH)

    for distance in (1, -1, 2, -2):
        greet(lat, along(distance))
    greet(lat, partner)
    greet(lat, team[2][0])

    for step in range(1, n_lat):
        greet((lat + step) % n_lat, z * 2)
        greet((lat + step) % n_lat, z * 2 + 1)

    for f in range(2):
        value = g_ref[:, f, :]
        high = value.astype(jnp.bfloat16).astype(jnp.float32)
        grid[f * DEG : f * DEG + ROWS, :] = high
        grid[64 + f * DEG : 64 + f * DEG + ROWS, :] = value - high
    down = jnp.transpose(grid[...])
    turn = jnp.where(iota(down.shape, 0) % 2 == 1, -1.0, 1.0)
    both[...] = jnp.concatenate([down, down * turn], axis=1).astype(jnp.bfloat16)

    for t in range(asg_ref.shape[0]):
        row = jnp.broadcast_to(asg_ref[t : t + 1, :].astype(jnp.float32), (LANES, LANES))
        asg_col[t * LANES : (t + 1) * LANES, :] = jnp.transpose(row)

    picked = 2 * dests
    lane = iota((picked, LANES), 1)
    tiles = -(-modes // LANES)
    entry = iota((picked, 2 * kept), 1)
    mirrored = nlon // 2 - (entry - kept)
    mode_of = jnp.where(entry < kept, entry, jnp.where(mirrored >= kept, mirrored, -1)).astype(jnp.float32)
    entry_tiles = -(-2 * kept // LANES)
    for kappa in range(KAPPA):
        wave = asg_col[pl.ds(kappa, picked, stride=KAPPA), :]
        wave = jnp.concatenate([wave] * entry_tiles, axis=1)[:, : 2 * kept]
        choice[kappa] = jnp.where(wave == mode_of, 1.0, 0.0).astype(jnp.bfloat16)

    for i, (c, begin, end) in enumerate(pieces):
        tab_copies[i].wait()
        part = dot(tab[c * kept + begin : c * kept + end, :], both[...])
        for turned in range(2):
            half_part = part[:, turned * LANES : (turned + 1) * LANES]
            total = half_part + pltpu.roll(half_part, 64, 1)
            if turned and c:
                total = -total
            begins = turned * kept + begin
            spec[begins : begins + end - begin, c * LANES : (c + 1) * LANES] = total.astype(jnp.bfloat16)

    packed = [[jnp.zeros((picked, LANES), jnp.float32) for _ in range(2)] for _ in range(2)]
    for kappa in range(KAPPA):
        chosen = dot(choice[kappa], spec[...])
        here = (lane >= kappa * ROWS) & (lane < (kappa + 1) * ROWS)
        for f in range(2):
            for c in range(2):
                moved = chosen[:, c * LANES : (c + 1) * LANES]
                shift = (kappa * ROWS - f * DEG) % LANES
                if shift:
                    moved = pltpu.roll(moved, shift, 1)
                packed[f][c] = jnp.where(here, moved, packed[f][c])
    for f in range(2):
        for c in range(2):
            send32[pl.ds(f * 2 + c, picked, stride=4), :] = packed[f][c]
    send[...] = send32[...].reshape(dests, 8, LANES).astype(jnp.bfloat16)

    pl.semaphore_wait(barrier, 2 * n_lat - 1 + 5)

    def block_to(target_lat, h):
        pltpu.make_async_remote_copy(
            src_ref=send.at[target_lat * 2 + h],
            dst_ref=recv.at[me],
            send_sem=a_send_sem,
            recv_sem=a_recv_sem,
            device_id={"lat": target_lat, "lev": z * 2 + h},
            device_id_type=MESH,
        ).start()

    def blocks_to(step, carry):
        target = (lat + step) % n_lat
        block_to(target, 0)
        block_to(target, 1)
        return carry

    lax.fori_loop(1, n_lat, blocks_to, 0)
    block_to(lat, other)
    own_block = pltpu.make_async_copy(send.at[me], recv.at[me], local_sem)
    own_block.start()

    for s in range(ROWS):
        leg32[s * DEG : s * DEG + ROWS, :] = leg_ref[s].astype(jnp.float32)
    for group in range(4):
        l_send[group] = leg32[group * OWN * DEG : (group + 1) * OWN * DEG, :].astype(jnp.bfloat16)
    l_copies = []
    for i, (device, group) in enumerate(team):
        copy = pltpu.make_async_remote_copy(
            src_ref=l_send.at[group], dst_ref=l_recv.at[i], send_sem=l_sems.at[i], recv_sem=l_sems.at[3 + i],
            device_id={"lat": lat, "lev": device}, device_id_type=MESH,
        )
        copy.start()
        l_copies.append(copy)

    row_of = iota((half, wide), 0)
    col_of = iota((half, wide), 1)
    mirror = jnp.where((row_of == col_of) | (row_of + col_of == wide - 1), 1.0, 0.0).astype(jnp.bfloat16)

    src = iota((n_z * 8, n_z * 8), 0)
    dst = iota((n_z * 8, n_z * 8), 1)
    position, inner = src // 8, src % 8
    distance = (position + 1) // 2
    from_z = jnp.where(position % 2 == 1, z - distance + n_z, z + distance) % n_z
    column = (inner % 2) * (n_z * 4) + from_z * 4 + inner // 2
    place = jnp.where(column == dst, 1.0, 0.0).astype(jnp.bfloat16)
    spread[0] = dot(l_send[home], mirror)

    pltpu.make_async_copy(recv.at[pl.ds(0, dests - 1)], recv.at[pl.ds(0, dests - 1)], a_recv_sem).wait()
    own_block.wait()
    low = iota((8, LANES), 0) < 4
    for i in range(n_lat):
        a = recv[2 * i].astype(jnp.float32)
        b = recv[2 * i + 1].astype(jnp.float32)
        mixed[0, i] = jnp.where(low, a, pltpu.roll(b, 4, 0))
        mixed[1, i] = jnp.where(low, pltpu.roll(a, 4, 0), b)

    lane = iota((8, LANES), 1)

    def side_by_side(u, kappa):
        parts = [jnp.zeros((8, LANES), jnp.float32) for _ in range(tiles)]
        for i in range(n_lat):
            start = i * ROWS
            t, offset = start // LANES, start % LANES
            value = mixed[u, i]
            shift = (offset - kappa * ROWS) % LANES
            if shift:
                value = pltpu.roll(value, shift, 1)
            parts[t] = jnp.where((lane >= offset) & (lane < offset + ROWS), value, parts[t])
            if offset + ROWS > LANES:
                parts[t + 1] = jnp.where(lane < offset + ROWS - LANES, value, parts[t + 1])
        return jnp.concatenate(parts, axis=1)[:, :wide].astype(jnp.bfloat16)

    def unit_copy(source, target, p, device):
        return pltpu.make_async_remote_copy(
            src_ref=source.at[CHUNKS[p]],
            dst_ref=units.at[target, CHUNKS[p]],
            send_sem=u_send_sem,
            recv_sem=u_recv_sem.at[target, p],
            device_id={"lat": lat, "lev": device},
            device_id_type=MESH,
        )

    last = n_z - 1
    turns = n_z // 2
    right, left = along(2), along(-2)

    def arrive_right(t, p):
        source = 2 * t - 1
        unit_copy(away, source, p, right).wait_recv()
        if t + 2 < turns:
            unit_copy(units.at[source], source + 4, p, right).start()
        elif t + 2 == turns and p == 0:
            unit_copy(units.at[source], last, p, right).start()

    def arrive_left(t, p):
        source = 2 * t
        unit_copy(away, source, p, left).wait_recv()
        if t + 2 < turns:
            unit_copy(units.at[source], source + 4, p, left).start()
        elif t + 2 == turns and p == 1:
            unit_copy(units.at[source], last, p, left).start()

    for p, chunk in enumerate(CHUNKS):
        for kappa in range(chunk.start, chunk.start + chunk.size):
            units[0, kappa] = side_by_side(odd, kappa)
        unit_copy(units.at[0], 3, p, right).start()
        unit_copy(units.at[0], 4, p, left).start()
        for kappa in range(chunk.start, chunk.start + chunk.size):
            away[kappa] = side_by_side(1 - odd, kappa)
        unit_copy(away, 1, p, along(1)).start()
        unit_copy(away, 2, p, along(-1)).start()

    for i in range(3):
        l_copies[i].wait()
        spread[1 + i] = dot(l_recv[i], mirror)
    degree = iota((DEG, wide), 0)
    sign = jnp.where((degree % 2 == 1) & (iota((DEG, wide), 1) >= half), -1.0, 1.0)
    degree = degree.astype(jnp.float32)
    for s in range(OWN):
        wave = asg_col[pl.ds(lat * ROWS + home * OWN + s, 1), :]
        wave = jnp.concatenate([wave] * tiles, axis=1)[:, :modes]
        rows = []
        for i, device in enumerate([lev] + [device for device, _ in team]):
            limit = jnp.minimum(modes - wave - (device * ROWS).astype(jnp.float32), float(ROWS))
            keep = degree < jnp.broadcast_to(limit, (DEG, wide))
            rows.append(jnp.where(keep, spread[i, s * DEG : (s + 1) * DEG, :] * sign, 0.0))
        factor[s] = jnp.concatenate(rows, axis=0).astype(jnp.bfloat16)

    def contract(s, begin, end):
        arrived = units[begin:end, s].astype(jnp.float32).reshape((end - begin) * 8, wide).astype(jnp.bfloat16)
        columns = dot_nt(factor[s], arrived).astype(jnp.bfloat16)
        return dot(columns, place[begin * 8 : end * 8])

    done = 0
    for t in range(1, turns):
        for p in range(2):
            arrive_right(t, p)
            arrive_left(t, p)
        if t in (turns - 2, turns - 1):
            end = (2 * t + 1) // 2 * 2
            for s in range(OWN):
                value = contract(s, done, end)
                first[s] = value if done == 0 else first[s] + value
            done = end
    for p, chunk in enumerate(CHUNKS):
        unit_copy(away, last, p, right).wait_recv()
        for s in range(chunk.start, chunk.start + chunk.size):
            product = first[s] + contract(s, done, n_z)
            out_ref[home * OWN + s] = product[:ROWS].astype(jnp.bfloat16)
            for i in range(3):
                p_send[i, s] = product[(1 + i) * DEG : (2 + i) * DEG].astype(jnp.bfloat16)

    p_copies = []
    for i in (2, 1, 0):
        copy = pltpu.make_async_remote_copy(
            src_ref=p_send.at[i], dst_ref=p_recv.at[i], send_sem=p_sems.at[i], recv_sem=p_sems.at[3 + i],
            device_id={"lat": lat, "lev": team[i][0]}, device_id_type=MESH,
        )
        copy.start()
        p_copies.append((i, copy))
    pltpu.make_async_copy(send.at[pl.ds(0, dests - 1)], send.at[pl.ds(0, dests - 1)], a_send_sem).wait()
    pltpu.make_async_copy(units.at[pl.ds(0, last)], units.at[pl.ds(0, last)], u_send_sem).wait()
    for i, copy in reversed(p_copies):
        copy.wait()
        for s in range(OWN):
            out_ref[team[i][1] * OWN + s] = p_recv[i, s][:ROWS, :]


def table_of(kept, nlon):
    phase = np.arange(kept, dtype=np.int64)[:, None] * np.arange(nlon, dtype=np.int64)[None, :] % nlon
    angle = phase * (2.0 * np.pi / nlon)
    weight = np.where(np.arange(kept) == 0, 1.0, 2.0)[:, None]
    return np.concatenate([np.cos(angle) * weight, -np.sin(angle) * weight], axis=0)


def per_device(n_lat, n_z, grid_gradient, legendre, assign):
    modes = n_lat * ROWS
    nlon = grid_gradient.shape[2]
    wide, half, dests = modes, modes // 2, 2 * n_lat
    tiles = -(-modes // LANES)
    kept = (nlon // 4 + 16) // 16 * 16
    table = jnp.asarray(table_of(kept, nlon).astype(jnp.bfloat16))
    rows = jnp.pad(assign, (0, tiles * LANES - modes)).reshape(tiles, LANES)
    vmem = pl.BlockSpec(memory_space=pltpu.VMEM)
    bf16, f32 = jnp.bfloat16, jnp.float32
    dma = pltpu.SemaphoreType.DMA
    result = pl.pallas_call(
        functools.partial(kernel, n_lat, n_z),
        out_shape=pltpu.VMEM((ROWS, ROWS, n_z * 8), bf16),
        in_specs=[vmem, vmem, vmem, pl.BlockSpec(memory_space=pltpu.MemorySpace.HBM)],
        out_specs=vmem,
        scratch_shapes=[
            pltpu.VMEM((2 * kept, nlon), bf16),
            pltpu.VMEM((LANES, nlon), f32),
            pltpu.VMEM((nlon, 2 * LANES), bf16),
            pltpu.VMEM((2 * kept, 2 * LANES), bf16),
            pltpu.VMEM((KAPPA, 2 * dests, 2 * kept), bf16),
            pltpu.VMEM((tiles * LANES, LANES), f32),
            pltpu.VMEM((dests * 8, LANES), f32),
            pltpu.VMEM((dests, 8, LANES), bf16),
            pltpu.VMEM((dests, 8, LANES), bf16),
            pltpu.VMEM((2, n_lat, 8, LANES), f32),
            pltpu.VMEM((ROWS * DEG, half), f32),
            pltpu.VMEM((4, OWN * DEG, half), bf16),
            pltpu.VMEM((3, OWN * DEG, half), bf16),
            pltpu.VMEM((4, OWN * DEG, wide), f32),
            pltpu.VMEM((OWN, 4 * DEG, wide), bf16),
            pltpu.VMEM((n_z, OWN, 8, wide), bf16),
            pltpu.VMEM((OWN, 8, wide), bf16),
            pltpu.VMEM((OWN, 4 * DEG, n_z * 8), f32),
            pltpu.VMEM((3, OWN, DEG, n_z * 8), bf16),
            pltpu.VMEM((3, OWN, DEG, n_z * 8), bf16),
            dma((4,)),
            dma,
            dma,
            dma,
            dma((6,)),
            dma((6,)),
            dma,
            dma((n_z, 2)),
        ],
        compiler_params=pltpu.CompilerParams(collective_id=0, has_side_effects=True),
        name="spectral_adjoint",
    )(jnp.transpose(grid_gradient, (1, 0, 2)), legendre, rows, table)

    def hand_on(result_ref, out_ref):
        out_ref[...] = result_ref[...]

    return pl.pallas_call(
        hand_on,
        out_shape=jax.ShapeDtypeStruct(result.shape, result.dtype),
        in_specs=[vmem],
        out_specs=vmem,
        name="hand_on",
    )(pltpu.with_memory_space_constraint(result, pltpu.VMEM))


def solution(mesh):
    in_specs = (P("lev", "lat", None), P("lat", "lev", None), P())
    out_specs = P("lat", "lev", None)
    body = functools.partial(per_device, mesh.shape["lat"], mesh.shape["lev"] // 2)
    return jax.shard_map(body, mesh=mesh, in_specs=in_specs, out_specs=out_specs, check_vma=False)
```

```python
import functools

import jax
import jax.numpy as jnp
import numpy as np
from jax import lax
from jax.experimental import pallas as pl
from jax.experimental.pallas import tpu as pltpu
from jax.sharding import PartitionSpec as P

MESH = pl.DeviceIdType.MESH
LANES = 128
ROWS = 20
KAPPA = 5
OWN = 5
CHUNKS = (pl.ds(0, 3), pl.ds(3, 2))
DEG = 24
NT = (((1,), (1,)), ((), ()))


def dot_nt(a, b):
    return lax.dot_general(a, b, NT, preferred_element_type=jnp.float32)


def dot(a, b):
    return jnp.dot(a, b, preferred_element_type=jnp.float32)


def iota(shape, axis):
    return lax.broadcasted_iota(jnp.int32, shape, axis)


def kernel(
    n_lat, n_z, g_ref, leg_hbm, asg_ref, tab_hbm, out_ref,
    tab, leg, grid, both, spec, choice, asg_col, send32, send, recv, mixed, leg32, l_send, l_recv, spread, factor, units, away, first,
    p_send, p_recv, tab_sem, a_send_sem, a_recv_sem, local_sem, l_sems, p_sems, u_send_sem, u_recv_sem, leg_sem,
):
    modes = n_lat * ROWS
    wide = modes
    half = wide // 2
    nlon = tab.shape[1]
    dests = 2 * n_lat
    lat = lax.axis_index("lat")
    lev = lax.axis_index("lev")
    z, core = lev // 2, lev % 2
    other = 1 - core
    odd = z % 2

    def along(distance):
        return ((z + distance + n_z) % n_z) * 2 + core

    twin = z + 1 - 2 * odd
    partner = z * 2 + other
    team = [(partner, other * 2 + odd), (twin * 2 + core, core * 2 + 1 - odd), (twin * 2 + other, other * 2 + 1 - odd)]
    home = core * 2 + odd
    me = lat * 2 + core

    kept = tab.shape[0] // 2
    split = kept // 32 * 16
    pieces = [(0, 0, split), (0, split, kept), (1, 0, split), (1, split, kept)]
    tab_copies = []
    for i, (c, begin, end) in enumerate(pieces):
        rows = pl.ds(c * kept + begin, end - begin)
        copy = pltpu.make_async_copy(tab_hbm.at[rows], tab.at[rows], tab_sem.at[i])
        copy.start()
        tab_copies.append(copy)
    leg_copy = pltpu.make_async_copy(leg_hbm, leg, leg_sem)
    leg_copy.start()

    barrier = pltpu.get_barrier_semaphore()

    def greet(target_lat, target_lev):
        pl.semaphore_signal(barrier, inc=1, device_id={"lat": target_lat, "lev": target_lev}, device_id_type=MESH)

    for distance in (1, -1, 2, -2):
        greet(lat, along(distance))
    greet(lat, partner)
    greet(lat, team[2][0])

    for step in range(1, n_lat):
        greet((lat + step) % n_lat, z * 2)
        greet((lat + step) % n_lat, z * 2 + 1)

    for f in range(2):
        value = g_ref[:, f, :]
        high = value.astype(jnp.bfloat16).astype(jnp.float32)
        grid[f * DEG : f * DEG + ROWS, :] = high
        grid[64 + f * DEG : 64 + f * DEG + ROWS, :] = value - high
    down = jnp.transpose(grid[...])
    turn = jnp.where(iota(down.shape, 0) % 2 == 1, -1.0, 1.0)
    both[...] = jnp.concatenate([down, down * turn], axis=1).astype(jnp.bfloat16)

    for t in range(asg_ref.shape[0]):
        row = jnp.broadcast_to(asg_ref[t : t + 1, :].astype(jnp.float32), (LANES, LANES))
        asg_col[t * LANES : (t + 1) * LANES, :] = jnp.transpose(row)

    picked = 2 * dests
    lane = iota((picked, LANES), 1)
    tiles = -(-modes // LANES)
    entry = iota((picked, 2 * kept), 1)
    mirrored = nlon // 2 - (entry - kept)
    mode_of = jnp.where(entry < kept, entry, jnp.where(mirrored >= kept, mirrored, -1)).astype(jnp.float32)
    entry_tiles = -(-2 * kept // LANES)
    for kappa in range(KAPPA):
        wave = asg_col[pl.ds(kappa, picked, stride=KAPPA), :]
        wave = jnp.concatenate([wave] * entry_tiles, axis=1)[:, : 2 * kept]
        choice[kappa] = jnp.where(wave == mode_of, 1.0, 0.0).astype(jnp.bfloat16)

    for i, (c, begin, end) in enumerate(pieces):
        tab_copies[i].wait()
        part = dot(tab[c * kept + begin : c * kept + end, :], both[...])
        for turned in range(2):
            half_part = part[:, turned * LANES : (turned + 1) * LANES]
            total = half_part + pltpu.roll(half_part, 64, 1)
            if turned and c:
                total = -total
            begins = turned * kept + begin
            spec[begins : begins + end - begin, c * LANES : (c + 1) * LANES] = total.astype(jnp.bfloat16)

    packed = [[jnp.zeros((picked, LANES), jnp.float32) for _ in range(2)] for _ in range(2)]
    for kappa in range(KAPPA):
        chosen = dot(choice[kappa], spec[...])
        here = (lane >= kappa * ROWS) & (lane < (kappa + 1) * ROWS)
        for f in range(2):
            for c in range(2):
                moved = chosen[:, c * LANES : (c + 1) * LANES]
                shift = (kappa * ROWS - f * DEG) % LANES
                if shift:
                    moved = pltpu.roll(moved, shift, 1)
                packed[f][c] = jnp.where(here, moved, packed[f][c])
    for f in range(2):
        for c in range(2):
            send32[pl.ds(f * 2 + c, picked, stride=4), :] = packed[f][c]
    send[...] = send32[...].reshape(dests, 8, LANES).astype(jnp.bfloat16)

    pl.semaphore_wait(barrier, 2 * n_lat - 1 + 5)

    def block_to(target_lat, h):
        pltpu.make_async_remote_copy(
            src_ref=send.at[target_lat * 2 + h],
            dst_ref=recv.at[me],
            send_sem=a_send_sem,
            recv_sem=a_recv_sem,
            device_id={"lat": target_lat, "lev": z * 2 + h},
            device_id_type=MESH,
        ).start()

    def blocks_to(step, carry):
        target = (lat + step) % n_lat
        block_to(target, 0)
        block_to(target, 1)
        return carry

    lax.fori_loop(1, n_lat, blocks_to, 0)
    block_to(lat, other)
    own_block = pltpu.make_async_copy(send.at[me], recv.at[me], local_sem)
    own_block.start()

    leg_copy.wait()
    for s in range(ROWS):
        leg32[s * DEG : s * DEG + ROWS, :] = leg[s].astype(jnp.float32)
    for group in range(4):
        l_send[group] = leg32[group * OWN * DEG : (group + 1) * OWN * DEG, :].astype(jnp.bfloat16)
    l_copies = []
    for i, (device, group) in enumerate(team):
        copy = pltpu.make_async_remote_copy(
            src_ref=l_send.at[group], dst_ref=l_recv.at[i], send_sem=l_sems.at[i], recv_sem=l_sems.at[3 + i],
            device_id={"lat": lat, "lev": device}, device_id_type=MESH,
        )
        copy.start()
        l_copies.append(copy)

    row_of = iota((half, wide), 0)
    col_of = iota((half, wide), 1)
    mirror = jnp.where((row_of == col_of) | (row_of + col_of == wide - 1), 1.0, 0.0).astype(jnp.bfloat16)

    src = iota((n_z * 8, n_z * 8), 0)
    dst = iota((n_z * 8, n_z * 8), 1)
    position, inner = src // 8, src % 8
    distance = (position + 1) // 2
    from_z = jnp.where(position % 2 == 1, z - distance + n_z, z + distance) % n_z
    column = (inner % 2) * (n_z * 4) + from_z * 4 + inner // 2
    place = jnp.where(column == dst, 1.0, 0.0).astype(jnp.bfloat16)
    spread[0] = dot(l_send[home], mirror)

    pltpu.make_async_copy(recv.at[pl.ds(0, dests - 1)], recv.at[pl.ds(0, dests - 1)], a_recv_sem).wait()
    own_block.wait()
    low = iota((8, LANES), 0) < 4
    for i in range(n_lat):
        a = recv[2 * i].astype(jnp.float32)
        b = recv[2 * i + 1].astype(jnp.float32)
        mixed[0, i] = jnp.where(low, a, pltpu.roll(b, 4, 0))
        mixed[1, i] = jnp.where(low, pltpu.roll(a, 4, 0), b)

    lane = iota((8, LANES), 1)

    def side_by_side(u, kappa):
        parts = [jnp.zeros((8, LANES), jnp.float32) for _ in range(tiles)]
        for i in range(n_lat):
            start = i * ROWS
            t, offset = start // LANES, start % LANES
            value = mixed[u, i]
            shift = (offset - kappa * ROWS) % LANES
            if shift:
                value = pltpu.roll(value, shift, 1)
            parts[t] = jnp.where((lane >= offset) & (lane < offset + ROWS), value, parts[t])
            if offset + ROWS > LANES:
                parts[t + 1] = jnp.where(lane < offset + ROWS - LANES, value, parts[t + 1])
        return jnp.concatenate(parts, axis=1)[:, :wide].astype(jnp.bfloat16)

    def unit_copy(source, target, p, device):
        return pltpu.make_async_remote_copy(
            src_ref=source.at[CHUNKS[p]],
            dst_ref=units.at[target, CHUNKS[p]],
            send_sem=u_send_sem,
            recv_sem=u_recv_sem.at[target, p],
            device_id={"lat": lat, "lev": device},
            device_id_type=MESH,
        )

    last = n_z - 1
    turns = n_z // 2
    right, left = along(2), along(-2)

    def arrive_right(t, p):
        source = 2 * t - 1
        unit_copy(away, source, p, right).wait_recv()
        if t + 2 < turns:
            unit_copy(units.at[source], source + 4, p, right).start()
        elif t + 2 == turns and p == 0:
            unit_copy(units.at[source], last, p, right).start()

    def arrive_left(t, p):
        source = 2 * t
        unit_copy(away, source, p, left).wait_recv()
        if t + 2 < turns:
            unit_copy(units.at[source], source + 4, p, left).start()
        elif t + 2 == turns and p == 1:
            unit_copy(units.at[source], last, p, left).start()

    for p, chunk in enumerate(CHUNKS):
        for kappa in range(chunk.start, chunk.start + chunk.size):
            units[0, kappa] = side_by_side(odd, kappa)
        unit_copy(units.at[0], 3, p, right).start()
        unit_copy(units.at[0], 4, p, left).start()
        for kappa in range(chunk.start, chunk.start + chunk.size):
            away[kappa] = side_by_side(1 - odd, kappa)
        unit_copy(away, 1, p, along(1)).start()
        unit_copy(away, 2, p, along(-1)).start()

    def prepare_factors():
        for i in range(3):
            l_copies[i].wait()
            spread[1 + i] = dot(l_recv[i], mirror)
        degree = iota((DEG, wide), 0)
        sign = jnp.where((degree % 2 == 1) & (iota((DEG, wide), 1) >= half), -1.0, 1.0)
        degree = degree.astype(jnp.float32)
        for s in range(OWN):
            wave = asg_col[pl.ds(lat * ROWS + home * OWN + s, 1), :]
            wave = jnp.concatenate([wave] * tiles, axis=1)[:, :modes]
            rows = []
            for i, device in enumerate([lev] + [device for device, _ in team]):
                limit = jnp.minimum(modes - wave - (device * ROWS).astype(jnp.float32), float(ROWS))
                keep = degree < jnp.broadcast_to(limit, (DEG, wide))
                rows.append(jnp.where(keep, spread[i, s * DEG : (s + 1) * DEG, :] * sign, 0.0))
            factor[s] = jnp.concatenate(rows, axis=0).astype(jnp.bfloat16)

    def contract(s, begin, end):
        arrived = units[begin:end, s].astype(jnp.float32).reshape((end - begin) * 8, wide).astype(jnp.bfloat16)
        columns = dot_nt(factor[s], arrived).astype(jnp.bfloat16)
        return dot(columns, place[begin * 8 : end * 8])

    done = 0
    for t in range(1, turns):
        for p in range(2):
            arrive_right(t, p)
            arrive_left(t, p)
        if t == 2:
            prepare_factors()
        if t in (turns - 2, turns - 1):
            end = (2 * t + 1) // 2 * 2
            for s in range(OWN):
                value = contract(s, done, end)
                first[s] = value if done == 0 else first[s] + value
            done = end
    for p, chunk in enumerate(CHUNKS):
        unit_copy(away, last, p, right).wait_recv()
        for s in range(chunk.start, chunk.start + chunk.size):
            product = first[s] + contract(s, done, n_z)
            out_ref[home * OWN + s] = product[:ROWS].astype(jnp.bfloat16)
            for i in range(3):
                p_send[i, s] = product[(1 + i) * DEG : (2 + i) * DEG].astype(jnp.bfloat16)

    p_copies = []
    for i in (2, 1, 0):
        copy = pltpu.make_async_remote_copy(
            src_ref=p_send.at[i], dst_ref=p_recv.at[i], send_sem=p_sems.at[i], recv_sem=p_sems.at[3 + i],
            device_id={"lat": lat, "lev": team[i][0]}, device_id_type=MESH,
        )
        copy.start()
        p_copies.append((i, copy))
    pltpu.make_async_copy(send.at[pl.ds(0, dests - 1)], send.at[pl.ds(0, dests - 1)], a_send_sem).wait()
    pltpu.make_async_copy(units.at[pl.ds(0, last)], units.at[pl.ds(0, last)], u_send_sem).wait()
    for i, copy in reversed(p_copies):
        copy.wait()
        for s in range(OWN):
            out_ref[team[i][1] * OWN + s] = p_recv[i, s][:ROWS, :]


def table_of(kept, nlon):
    phase = np.arange(kept, dtype=np.int64)[:, None] * np.arange(nlon, dtype=np.int64)[None, :] % nlon
    angle = phase * (2.0 * np.pi / nlon)
    weight = np.where(np.arange(kept) == 0, 1.0, 2.0)[:, None]
    return np.concatenate([np.cos(angle) * weight, -np.sin(angle) * weight], axis=0)


def per_device(n_lat, n_z, grid_gradient, legendre, assign):
    modes = n_lat * ROWS
    nlon = grid_gradient.shape[2]
    wide, half, dests = modes, modes // 2, 2 * n_lat
    tiles = -(-modes // LANES)
    kept = (nlon // 4 + 16) // 16 * 16
    table = jnp.asarray(table_of(kept, nlon).astype(jnp.bfloat16))
    rows = jnp.pad(assign, (0, tiles * LANES - modes)).reshape(tiles, LANES)
    vmem = pl.BlockSpec(memory_space=pltpu.VMEM)
    hbm = pl.BlockSpec(memory_space=pltpu.MemorySpace.HBM)
    bf16, f32 = jnp.bfloat16, jnp.float32
    dma = pltpu.SemaphoreType.DMA
    result = pl.pallas_call(
        functools.partial(kernel, n_lat, n_z),
        out_shape=pltpu.VMEM((ROWS, ROWS, n_z * 8), bf16),
        in_specs=[vmem, hbm, vmem, hbm],
        out_specs=vmem,
        scratch_shapes=[
            pltpu.VMEM((2 * kept, nlon), bf16),
            pltpu.VMEM((ROWS, ROWS, half), bf16),
            pltpu.VMEM((LANES, nlon), f32),
            pltpu.VMEM((nlon, 2 * LANES), bf16),
            pltpu.VMEM((2 * kept, 2 * LANES), bf16),
            pltpu.VMEM((KAPPA, 2 * dests, 2 * kept), bf16),
            pltpu.VMEM((tiles * LANES, LANES), f32),
            pltpu.VMEM((dests * 8, LANES), f32),
            pltpu.VMEM((dests, 8, LANES), bf16),
            pltpu.VMEM((dests, 8, LANES), bf16),
            pltpu.VMEM((2, n_lat, 8, LANES), f32),
            pltpu.VMEM((ROWS * DEG, half), f32),
            pltpu.VMEM((4, OWN * DEG, half), bf16),
            pltpu.VMEM((3, OWN * DEG, half), bf16),
            pltpu.VMEM((4, OWN * DEG, wide), f32),
            pltpu.VMEM((OWN, 4 * DEG, wide), bf16),
            pltpu.VMEM((n_z, OWN, 8, wide), bf16),
            pltpu.VMEM((OWN, 8, wide), bf16),
            pltpu.VMEM((OWN, 4 * DEG, n_z * 8), f32),
            pltpu.VMEM((3, OWN, DEG, n_z * 8), bf16),
            pltpu.VMEM((3, OWN, DEG, n_z * 8), bf16),
            dma((4,)),
            dma,
            dma,
            dma,
            dma((6,)),
            dma((6,)),
            dma,
            dma((n_z, 2)),
            dma,
        ],
        compiler_params=pltpu.CompilerParams(collective_id=0, has_side_effects=True),
        name="spectral_adjoint",
    )(jnp.transpose(grid_gradient, (1, 0, 2)), legendre, rows, table)

    def hand_on(result_ref, out_ref):
        out_ref[...] = result_ref[...]

    return pl.pallas_call(
        hand_on,
        out_shape=jax.ShapeDtypeStruct(result.shape, result.dtype),
        in_specs=[vmem],
        out_specs=vmem,
        name="hand_on",
    )(pltpu.with_memory_space_constraint(result, pltpu.VMEM))


def solution(mesh):
    in_specs = (P("lev", "lat", None), P("lat", "lev", None), P())
    out_specs = P("lat", "lev", None)
    body = functools.partial(per_device, mesh.shape["lat"], mesh.shape["lev"] // 2)
    return jax.shard_map(body, mesh=mesh, in_specs=in_specs, out_specs=out_specs, check_vma=False)
```

```python
import functools

import jax
import jax.numpy as jnp
import numpy as np
from jax import lax
from jax.experimental import pallas as pl
from jax.experimental.pallas import tpu as pltpu
from jax.sharding import PartitionSpec as P

MESH = pl.DeviceIdType.MESH
LANES = 128
ROWS = 20
KAPPA = 5
OWN = 5
CHUNKS = (pl.ds(0, 3), pl.ds(3, 2))
DEG = 24
NT = (((1,), (1,)), ((), ()))


def dot_nt(a, b):
    return lax.dot_general(a, b, NT, preferred_element_type=jnp.float32)


def dot(a, b):
    return jnp.dot(a, b, preferred_element_type=jnp.float32)


def iota(shape, axis):
    return lax.broadcasted_iota(jnp.int32, shape, axis)


def kernel(
    n_lat, n_z, g_ref, leg_hbm, asg_ref, tab_hbm, out_ref,
    tab, leg, grid, both, spec, choice, asg_col, send32, send, recv, mixed, leg32, l_send, l_recv, spread, factor, units, away, first,
    p_send, p_recv, tab_sem, a_send_sem, a_recv_sem, local_sem, l_sems, p_sems, u_send_sem, u_recv_sem, leg_sem,
):
    modes = n_lat * ROWS
    wide = modes
    half = wide // 2
    nlon = tab.shape[1]
    dests = 2 * n_lat
    lat = lax.axis_index("lat")
    lev = lax.axis_index("lev")
    z, core = lev // 2, lev % 2
    other = 1 - core
    odd = z % 2

    def along(distance):
        return ((z + distance + n_z) % n_z) * 2 + core

    twin = z + 1 - 2 * odd
    partner = z * 2 + other
    team = [(partner, other * 2 + odd), (twin * 2 + core, core * 2 + 1 - odd), (twin * 2 + other, other * 2 + 1 - odd)]
    home = core * 2 + odd
    me = lat * 2 + core

    kept = tab.shape[0] // 2
    split = kept // 32 * 16
    pieces = [(0, 0, split), (0, split, kept), (1, 0, split), (1, split, kept)]
    tab_copies = []
    for i, (c, begin, end) in enumerate(pieces):
        rows = pl.ds(c * kept + begin, end - begin)
        copy = pltpu.make_async_copy(tab_hbm.at[rows], tab.at[rows], tab_sem.at[i])
        copy.start()
        tab_copies.append(copy)
    leg_copy = pltpu.make_async_copy(leg_hbm, leg, leg_sem)
    leg_copy.start()

    barrier = pltpu.get_barrier_semaphore()

    def greet(target_lat, target_lev):
        pl.semaphore_signal(barrier, inc=1, device_id={"lat": target_lat, "lev": target_lev}, device_id_type=MESH)

    for distance in (1, -1, 2, -2):
        greet(lat, along(distance))
    greet(lat, partner)
    greet(lat, team[2][0])

    for step in range(1, n_lat):
        greet((lat + step) % n_lat, z * 2)
        greet((lat + step) % n_lat, z * 2 + 1)

    for f in range(2):
        value = g_ref[:, f, :]
        high = value.astype(jnp.bfloat16).astype(jnp.float32)
        grid[f * DEG : f * DEG + ROWS, :] = high
        grid[64 + f * DEG : 64 + f * DEG + ROWS, :] = value - high
    down = jnp.transpose(grid[...])
    turn = jnp.where(iota(down.shape, 0) % 2 == 1, -1.0, 1.0)
    both[...] = jnp.concatenate([down, down * turn], axis=1).astype(jnp.bfloat16)

    for t in range(asg_ref.shape[0]):
        row = jnp.broadcast_to(asg_ref[t : t + 1, :].astype(jnp.float32), (LANES, LANES))
        asg_col[t * LANES : (t + 1) * LANES, :] = jnp.transpose(row)

    picked = 2 * dests
    lane = iota((picked, LANES), 1)
    tiles = -(-modes // LANES)
    entry = iota((picked, 2 * kept), 1)
    mirrored = nlon // 2 - (entry - kept)
    mode_of = jnp.where(entry < kept, entry, jnp.where(mirrored >= kept, mirrored, -1)).astype(jnp.float32)
    entry_tiles = -(-2 * kept // LANES)
    for kappa in range(KAPPA):
        wave = asg_col[pl.ds(kappa, picked, stride=KAPPA), :]
        wave = jnp.concatenate([wave] * entry_tiles, axis=1)[:, : 2 * kept]
        choice[kappa] = jnp.where(wave == mode_of, 1.0, 0.0).astype(jnp.bfloat16)

    for i, (c, begin, end) in enumerate(pieces):
        tab_copies[i].wait()
        part = dot(tab[c * kept + begin : c * kept + end, :], both[...])
        for turned in range(2):
            half_part = part[:, turned * LANES : (turned + 1) * LANES]
            total = half_part + pltpu.roll(half_part, 64, 1)
            if turned and c:
                total = -total
            begins = turned * kept + begin
            spec[begins : begins + end - begin, c * LANES : (c + 1) * LANES] = total.astype(jnp.bfloat16)

    packed = [[jnp.zeros((picked, LANES), jnp.float32) for _ in range(2)] for _ in range(2)]
    for kappa in range(KAPPA):
        chosen = dot(choice[kappa], spec[...])
        here = (lane >= kappa * ROWS) & (lane < (kappa + 1) * ROWS)
        for f in range(2):
            for c in range(2):
                moved = chosen[:, c * LANES : (c + 1) * LANES]
                shift = (kappa * ROWS - f * DEG) % LANES
                if shift:
                    moved = pltpu.roll(moved, shift, 1)
                packed[f][c] = jnp.where(here, moved, packed[f][c])
    for f in range(2):
        for c in range(2):
            send32[pl.ds(f * 2 + c, picked, stride=4), :] = packed[f][c]
    send[...] = send32[...].reshape(dests, 8, LANES).astype(jnp.bfloat16)

    pl.semaphore_wait(barrier, 2 * n_lat - 1 + 5)

    def block_to(target_lat, h):
        pltpu.make_async_remote_copy(
            src_ref=send.at[target_lat * 2 + h],
            dst_ref=recv.at[me],
            send_sem=a_send_sem,
            recv_sem=a_recv_sem,
            device_id={"lat": target_lat, "lev": z * 2 + h},
            device_id_type=MESH,
        ).start()

    def blocks_to(step, carry):
        target = (lat + step) % n_lat
        block_to(target, 0)
        block_to(target, 1)
        return carry

    lax.fori_loop(1, n_lat, blocks_to, 0)
    block_to(lat, other)
    own_block = pltpu.make_async_copy(send.at[me], recv.at[me], local_sem)
    own_block.start()

    leg_copy.wait()
    for s in range(ROWS):
        leg32[s * DEG : s * DEG + ROWS, :] = leg[s].astype(jnp.float32)
    for group in range(4):
        l_send[group] = leg32[group * OWN * DEG : (group + 1) * OWN * DEG, :].astype(jnp.bfloat16)
    l_copies = []
    for i, (device, group) in enumerate(team):
        copy = pltpu.make_async_remote_copy(
            src_ref=l_send.at[group], dst_ref=l_recv.at[i], send_sem=l_sems.at[i], recv_sem=l_sems.at[3 + i],
            device_id={"lat": lat, "lev": device}, device_id_type=MESH,
        )
        copy.start()
        l_copies.append(copy)

    row_of = iota((half, wide), 0)
    col_of = iota((half, wide), 1)
    mirror = jnp.where((row_of == col_of) | (row_of + col_of == wide - 1), 1.0, 0.0).astype(jnp.bfloat16)

    src = iota((n_z * 8, n_z * 8), 0)
    dst = iota((n_z * 8, n_z * 8), 1)
    position, inner = src // 8, src % 8
    distance = (position + 1) // 2
    from_z = jnp.where(position % 2 == 1, z - distance + n_z, z + distance) % n_z
    column = (inner % 2) * (n_z * 4) + from_z * 4 + inner // 2
    place = jnp.where(column == dst, 1.0, 0.0).astype(jnp.bfloat16)
    spread[0] = dot(l_send[home], mirror)

    pltpu.make_async_copy(recv.at[pl.ds(0, dests - 1)], recv.at[pl.ds(0, dests - 1)], a_recv_sem).wait()
    own_block.wait()
    low = iota((8, LANES), 0) < 4
    for i in range(n_lat):
        a = recv[2 * i].astype(jnp.float32)
        b = recv[2 * i + 1].astype(jnp.float32)
        mixed[0, i] = jnp.where(low, a, pltpu.roll(b, 4, 0))
        mixed[1, i] = jnp.where(low, pltpu.roll(a, 4, 0), b)

    lane = iota((8, LANES), 1)

    def side_by_side(u, kappa):
        parts = [jnp.zeros((8, LANES), jnp.float32) for _ in range(tiles)]
        for i in range(n_lat):
            start = i * ROWS
            t, offset = start // LANES, start % LANES
            value = mixed[u, i]
            shift = (offset - kappa * ROWS) % LANES
            if shift:
                value = pltpu.roll(value, shift, 1)
            parts[t] = jnp.where((lane >= offset) & (lane < offset + ROWS), value, parts[t])
            if offset + ROWS > LANES:
                parts[t + 1] = jnp.where(lane < offset + ROWS - LANES, value, parts[t + 1])
        return jnp.concatenate(parts, axis=1)[:, :wide].astype(jnp.bfloat16)

    def unit_copy(source, target, p, device):
        return pltpu.make_async_remote_copy(
            src_ref=source.at[CHUNKS[p]],
            dst_ref=units.at[target, CHUNKS[p]],
            send_sem=u_send_sem,
            recv_sem=u_recv_sem.at[target, p],
            device_id={"lat": lat, "lev": device},
            device_id_type=MESH,
        )

    last = n_z - 1
    turns = n_z // 2
    right, left = along(2), along(-2)

    def arrive_right(t, p):
        source = 2 * t - 1
        unit_copy(away, source, p, right).wait_recv()
        if t + 2 < turns:
            unit_copy(units.at[source], source + 4, p, right).start()
        elif t + 2 == turns and p == 0:
            unit_copy(units.at[source], last, p, right).start()

    def arrive_left(t, p):
        source = 2 * t
        unit_copy(away, source, p, left).wait_recv()
        if t + 2 < turns:
            unit_copy(units.at[source], source + 4, p, left).start()
        elif t + 2 == turns and p == 1:
            unit_copy(units.at[source], last, p, left).start()

    for p, chunk in enumerate(CHUNKS):
        for kappa in range(chunk.start, chunk.start + chunk.size):
            units[0, kappa] = side_by_side(odd, kappa)
        unit_copy(units.at[0], 3, p, right).start()
        unit_copy(units.at[0], 4, p, left).start()
        for kappa in range(chunk.start, chunk.start + chunk.size):
            away[kappa] = side_by_side(1 - odd, kappa)
        unit_copy(away, 1, p, along(1)).start()
        unit_copy(away, 2, p, along(-1)).start()

    def prepare_factors():
        for i in range(3):
            l_copies[i].wait()
            spread[1 + i] = dot(l_recv[i], mirror)
        degree = iota((DEG, wide), 0)
        sign = jnp.where((degree % 2 == 1) & (iota((DEG, wide), 1) >= half), -1.0, 1.0)
        degree = degree.astype(jnp.float32)
        for s in range(OWN):
            wave = asg_col[pl.ds(lat * ROWS + home * OWN + s, 1), :]
            wave = jnp.concatenate([wave] * tiles, axis=1)[:, :modes]
            rows = []
            for i, device in enumerate([lev] + [device for device, _ in team]):
                limit = jnp.minimum(modes - wave - (device * ROWS).astype(jnp.float32), float(ROWS))
                keep = degree < jnp.broadcast_to(limit, (DEG, wide))
                rows.append(jnp.where(keep, spread[i, s * DEG : (s + 1) * DEG, :] * sign, 0.0))
            factor[s] = jnp.concatenate(rows, axis=0).astype(jnp.bfloat16)

    def contract(s, begin, end):
        arrived = units[begin:end, s].astype(jnp.float32).reshape((end - begin) * 8, wide).astype(jnp.bfloat16)
        columns = dot_nt(factor[s], arrived).astype(jnp.bfloat16)
        return dot(columns, place[begin * 8 : end * 8])

    done = 0
    for t in range(1, turns):
        for p in range(2):
            arrive_right(t, p)
            arrive_left(t, p)
        if t == 2:
            prepare_factors()
        if t in (turns - 2, turns - 1):
            end = (2 * t + 1) // 2 * 2
            for s in range(OWN):
                value = contract(s, done, end)
                first[s] = value if done == 0 else first[s] + value
            done = end
    p_copies = []
    for p, chunk in enumerate(CHUNKS):
        unit_copy(away, last, p, right).wait_recv()
        for s in range(chunk.start, chunk.start + chunk.size):
            product = first[s] + contract(s, done, n_z)
            out_ref[home * OWN + s] = product[:ROWS].astype(jnp.bfloat16)
            for i in range(3):
                p_send[i, s] = product[(1 + i) * DEG : (2 + i) * DEG].astype(jnp.bfloat16)
        for i in (2, 1, 0):
            copy = pltpu.make_async_remote_copy(
                src_ref=p_send.at[i, chunk], dst_ref=p_recv.at[i, chunk],
                send_sem=p_sems.at[p, i], recv_sem=p_sems.at[p, 3 + i],
                device_id={"lat": lat, "lev": team[i][0]}, device_id_type=MESH,
            )
            copy.start()
            p_copies.append((i, chunk, copy))


    pltpu.make_async_copy(send.at[pl.ds(0, dests - 1)], send.at[pl.ds(0, dests - 1)], a_send_sem).wait()
    pltpu.make_async_copy(units.at[pl.ds(0, last)], units.at[pl.ds(0, last)], u_send_sem).wait()
    for i, chunk, copy in p_copies:
        copy.wait()
        for s in range(chunk.start, chunk.start + chunk.size):
            out_ref[team[i][1] * OWN + s] = p_recv[i, s][:ROWS, :]


def table_of(kept, nlon):
    phase = np.arange(kept, dtype=np.int64)[:, None] * np.arange(nlon, dtype=np.int64)[None, :] % nlon
    angle = phase * (2.0 * np.pi / nlon)
    weight = np.where(np.arange(kept) == 0, 1.0, 2.0)[:, None]
    return np.concatenate([np.cos(angle) * weight, -np.sin(angle) * weight], axis=0)


def per_device(n_lat, n_z, grid_gradient, legendre, assign):
    modes = n_lat * ROWS
    nlon = grid_gradient.shape[2]
    wide, half, dests = modes, modes // 2, 2 * n_lat
    tiles = -(-modes // LANES)
    kept = (nlon // 4 + 16) // 16 * 16
    table = jnp.asarray(table_of(kept, nlon).astype(jnp.bfloat16))
    rows = jnp.pad(assign, (0, tiles * LANES - modes)).reshape(tiles, LANES)
    vmem = pl.BlockSpec(memory_space=pltpu.VMEM)
    hbm = pl.BlockSpec(memory_space=pltpu.MemorySpace.HBM)
    bf16, f32 = jnp.bfloat16, jnp.float32
    dma = pltpu.SemaphoreType.DMA
    result = pl.pallas_call(
        functools.partial(kernel, n_lat, n_z),
        out_shape=pltpu.VMEM((ROWS, ROWS, n_z * 8), bf16),
        in_specs=[vmem, hbm, vmem, hbm],
        out_specs=vmem,
        scratch_shapes=[
            pltpu.VMEM((2 * kept, nlon), bf16),
            pltpu.VMEM((ROWS, ROWS, half), bf16),
            pltpu.VMEM((LANES, nlon), f32),
            pltpu.VMEM((nlon, 2 * LANES), bf16),
            pltpu.VMEM((2 * kept, 2 * LANES), bf16),
            pltpu.VMEM((KAPPA, 2 * dests, 2 * kept), bf16),
            pltpu.VMEM((tiles * LANES, LANES), f32),
            pltpu.VMEM((dests * 8, LANES), f32),
            pltpu.VMEM((dests, 8, LANES), bf16),
            pltpu.VMEM((dests, 8, LANES), bf16),
            pltpu.VMEM((2, n_lat, 8, LANES), f32),
            pltpu.VMEM((ROWS * DEG, half), f32),
            pltpu.VMEM((4, OWN * DEG, half), bf16),
            pltpu.VMEM((3, OWN * DEG, half), bf16),
            pltpu.VMEM((4, OWN * DEG, wide), f32),
            pltpu.VMEM((OWN, 4 * DEG, wide), bf16),
            pltpu.VMEM((n_z, OWN, 8, wide), bf16),
            pltpu.VMEM((OWN, 8, wide), bf16),
            pltpu.VMEM((OWN, 4 * DEG, n_z * 8), f32),
            pltpu.VMEM((3, OWN, DEG, n_z * 8), bf16),
            pltpu.VMEM((3, OWN, DEG, n_z * 8), bf16),
            dma((4,)),
            dma,
            dma,
            dma,
            dma((6,)),
            dma((2, 6)),
            dma,
            dma((n_z, 2)),
            dma,
        ],
        compiler_params=pltpu.CompilerParams(collective_id=0, has_side_effects=True),
        name="spectral_adjoint",
    )(jnp.transpose(grid_gradient, (1, 0, 2)), legendre, rows, table)

    def hand_on(result_ref, out_ref):
        out_ref[...] = result_ref[...]

    return pl.pallas_call(
        hand_on,
        out_shape=jax.ShapeDtypeStruct(result.shape, result.dtype),
        in_specs=[vmem],
        out_specs=vmem,
        name="hand_on",
    )(pltpu.with_memory_space_constraint(result, pltpu.VMEM))


def solution(mesh):
    in_specs = (P("lev", "lat", None), P("lat", "lev", None), P())
    out_specs = P("lat", "lev", None)
    body = functools.partial(per_device, mesh.shape["lat"], mesh.shape["lev"] // 2)
    return jax.shard_map(body, mesh=mesh, in_specs=in_specs, out_specs=out_specs, check_vma=False)
```
